128 devices in a mesh: gx: 4 (over y), gy: 8 (over z, core), row: 4 (over x).
Axes of the slice: x: 4, y: 4, z: 4, core: 2. Of those that a mesh axis runs over, the one named last changes fastest.
Arguments:
- occupancy: int32 [32, 512, 4096], P('row', 'gx', 'gy'), may hold values 0 or 1
- random_draws: bfloat16 [4, 32, 512, 4096], P(None, 'row', 'gx', 'gy'), may hold values from 0 to 1
Outputs:
- coverage: float32 [128, 1024], P('gx', 'gy')
- projected: float32 [128, 1024], P('gx', 'gy')
The draws below stay inside these ranges and needn't reach their ends.
All inputs are finite; a program needn't handle non-finite values. No bound on the sum of `occupancy` on one device may be relied on, other than what follows from the above.
Results may differ from the reference program's by a relative error of at most 0.0003.
Values may be sent and summed in bfloat16 or wider, within the bound.
A program may use at most 64 MiB of HBM per device.

```python
import jax
import jax.numpy as jnp
from jax import lax

SWEEPS = 4
BLOCK = 4
LEAP = 8
NX = 512
NY = 4096
REAL = 32


def touch_ends(entries, own_key, smallest, top_value):
    extent = entries.shape
    index_at = [jax.random.randint(jax.random.fold_in(own_key, axis), (), 0, extent[axis]) for axis in range(len(extent))]
    entries = entries.at[tuple(index_at)].set(smallest)
    longest = extent.index(max(extent))
    index_at[longest] = (index_at[longest] + 1) % extent[longest]
    return entries.at[tuple(index_at)].set(top_value)


def levels(own_key, extent, shards, smallest, largest):
    gain, own = 1.0, jax.random.fold_in(own_key, 6)
    for position, blocks in shards:
        draws = jnp.exp(jax.random.uniform(jax.random.fold_in(own, position), (blocks,), jnp.float32, smallest / len(shards), largest / len(shards)))
        gain = gain * jnp.repeat(draws, extent[position] // blocks).reshape([-1 if axis == position else 1 for axis in range(len(extent))])
    return gain


def setup_inputs(seed: int = 0) -> dict:
    key_list = jax.random.split(jax.random.key(seed), 3)
    return {
        "occupancy": touch_ends((jax.random.randint(key_list[0], (REAL, NX, NY), 0, 2) < 1).astype(jnp.int32), jax.random.fold_in(key_list[0], 1), 0, 1),
        "random_draws": jnp.clip(1.0 * jax.random.uniform(key_list[1], (SWEEPS, REAL, NX, NY), jnp.float32) ** levels(key_list[1], (SWEEPS, REAL, NX, NY), ((1, 4), (2, 4), (3, 8)), -0.2, 0.2), 0.0, 1.0).astype(jnp.bfloat16),
    }


ADSORB = 0.6
DESORB = 0.6
HOPPING = 0.3
COUPLING = 0.5


def sublattice_update(padded, jitter, colour):
    centre = padded[..., 1:-1, 1:-1]
    beside = padded[..., 2:, 1:-1] + padded[..., :-2, 1:-1] + padded[..., 1:-1, 2:] + padded[..., 1:-1, :-2]
    updated = centre + ADSORB * jitter * (1.0 - centre) - DESORB * (1.0 - jitter) * jnp.exp(-COUPLING * beside) * centre + HOPPING * (0.25 * beside - centre)
    row_index = lax.broadcasted_iota(jnp.int32, centre.shape[-2:], 0)
    col_index = lax.broadcasted_iota(jnp.int32, centre.shape[-2:], 1)
    chosen = ((row_index + col_index + colour) % 2) == 0
    return jnp.where(chosen, updated, centre)


def block_sums(field):
    height, width = field.shape[-2], field.shape[-1]
    shaped = field.reshape(field.shape[:-2] + (height // BLOCK, BLOCK, width // BLOCK, BLOCK))
    return jnp.sum(shaped, axis=(-3, -1))


def one_realization(index, occupancy, random_draws):
    occupied = occupancy[index].astype(jnp.float32)
    earlier = occupied
    for sweep_index in range(SWEEPS):
        if sweep_index == SWEEPS - 2:
            earlier = occupied
        padded = jnp.pad(occupied, 1, mode="wrap")
        occupied = sublattice_update(padded, random_draws[sweep_index, index].astype(jnp.float32), sweep_index % 2)
    return jnp.stack([block_sums(earlier), block_sums(occupied)])


def reference(occupancy, random_draws):
    def mapped(index):
        return one_realization(index, occupancy, random_draws)
    coarse_each = lax.map(mapped, jnp.arange(REAL, dtype=jnp.int32))
    averages = jnp.sum(coarse_each, axis=0) / jnp.float32(REAL * BLOCK * BLOCK)
    coverage = averages[1]
    projected = coverage + (LEAP / 2.0) * (coverage - averages[0])
    return coverage, projected
```

```python
import functools

import jax
import jax.numpy as jnp
import numpy as np
from jax import lax
from jax.experimental import pallas as pl
from jax.experimental.pallas import tpu as pltpu
from jax.sharding import PartitionSpec as P

MESH = pl.DeviceIdType.MESH
BLOCK = 4
LEAP = 8
SCALE = float(-0.5 * np.log2(np.e))
F32 = jnp.float32
BF16 = jnp.bfloat16


def iota(shape, dim):
    return lax.broadcasted_iota(jnp.int32, shape, dim)


def new_value(x, total, u):
    gone = 0.6 - 0.6 * jnp.exp2(total)
    kept = x * gone
    return (0.1 * x + kept) + u * (0.6 * SCALE - kept) + 0.075 * total


def split_dot(x, onehot):
    high = x.astype(BF16)
    low = (x - high.astype(F32)).astype(BF16)
    return jnp.dot(high, onehot, preferred_element_type=F32) + jnp.dot(
        low, onehot, preferred_element_type=F32
    )


def split_dot_left(onehot, x):
    high = x.astype(BF16)
    low = (x - high.astype(F32)).astype(BF16)
    return jnp.dot(onehot, high, preferred_element_type=F32) + jnp.dot(
        onehot, low, preferred_element_type=F32
    )


def kernel(
    sizes,
    occ_hbm,
    u_hbm,
    cov_ref,
    proj_ref,
    occ,
    draws,
    st,
    uu,
    sums,
    rs,
    ub,
    rsums,
    cs,
    ucs,
    merged,
    side,
    vert_send,
    vert,
    diag,
    red_send,
    red,
    load_sem,
    send_sem,
    recv_sem,
    red_send_sem,
    red_recv_sem,
):
    ngx, ngy, nrow = sizes
    gx, gy, row = lax.axis_index("gx"), lax.axis_index("gy"), lax.axis_index("row")
    up, down = lax.rem(gx + ngx - 1, ngx), lax.rem(gx + 1, ngx)
    left, right = lax.rem(gy + ngy - 1, ngy), lax.rem(gy + 1, ngy)

    def load(pair):
        return (
            pltpu.make_async_copy(
                occ_hbm.at[pl.ds(2 * pair, 2)], occ.at[pl.ds(2 * pair, 2)], load_sem.at[0, pair]
            ),
            pltpu.make_async_copy(
                u_hbm.at[:, pl.ds(2 * pair, 2)],
                draws.at[:, pl.ds(2 * pair, 2)],
                load_sem.at[1, pair],
            ),
        )

    for pair in range(4):
        for copy in load(pair):
            copy.start()

    barrier = pltpu.get_barrier_semaphore()
    lattice = [
        (gx, left),
        (gx, right),
        (up, gy),
        (down, gy),
        (up, left),
        (up, right),
        (down, left),
        (down, right),
    ]
    for a, b in lattice:
        pl.semaphore_signal(barrier, inc=1, device_id=(a, b, row), device_id_type=MESH)
    peers = [lax.rem(row + d, nrow) for d in range(1, nrow)]
    for peer in peers:
        pl.semaphore_signal(barrier, inc=1, device_id=(gx, gy, peer), device_id_type=MESH)

    zeros8 = jnp.zeros((8, 128), F32)
    for which in range(2):
        for pair in range(4):
            for t in range(4):
                st[which, pair, t, 0:8, :] = zeros8
                st[which, pair, t, 136:144, :] = zeros8
                rs[which, pair, t, 0:8, :] = zeros8
                rs[which, pair, t, 32:40, :] = zeros8
        cs[which, 0:8, :] = zeros8
        cs[which, 152:160, :] = zeros8

    wide_even = ((iota((16, 512), 0) + iota((16, 512), 1)) % 2) == 0
    for pair in range(4):
        for copy in load(pair):
            copy.wait()

        def pack(c, carry, pair=pair):
            at = pl.multiple_of(c * 16, 16)
            first = occ[2 * pair, pl.ds(at, 16), :].astype(F32) * SCALE
            second = pltpu.roll(occ[2 * pair + 1, pl.ds(at, 16), :].astype(F32) * SCALE, 511, 1)
            both = (
                jnp.where(wide_even, first, second),
                jnp.where(wide_even, second, first),
            )
            for which in range(2):
                for t in range(4):
                    st[which, pair, t, pl.ds(8 + at, 16), :] = both[which][:, 128 * t : 128 * t + 128]
            for s in range(4):
                first = draws[s, 2 * pair, pl.ds(at, 16), :].astype(F32)
                second = pltpu.roll(draws[s, 2 * pair + 1, pl.ds(at, 16), :].astype(F32), 511, 1)
                chosen = (
                    jnp.where(wide_even, first, second)
                    if s % 2 == 0
                    else jnp.where(wide_even, second, first)
                )
                for t in range(4):
                    uu[s, pair, t, pl.ds(at, 16), :] = chosen[:, 128 * t : 128 * t + 128]
            return carry

        lax.fori_loop(0, 8, pack, 0)

    def source(q, pair, t, at, size):
        if q < 2:
            return st[q, pair, t, pl.ds(8 + at, size), :] * (1.0 / SCALE)
        return uu[q - 2, pair, t, pl.ds(at, size), :]

    def lanes(rows):
        lane = iota((rows, 128), 1)
        even = ((iota((rows, 128), 0) + lane) % 2) == 0
        return lane, lane % 32, even

    def merge(c, carry):
        at = pl.multiple_of(c * 16, 16)
        lane, small, even = lanes(16)
        for q in range(6):
            real0 = even if q % 2 == 0 else jnp.logical_not(even)
            early = jnp.logical_or(small < 15, jnp.logical_and(small == 15, real0))
            total = None
            for pair in range(4):
                edge = jnp.where(lane >= 64, source(q, pair, 3, at, 16), source(q, pair, 0, at, 16))
                one = jnp.where(
                    early,
                    pltpu.roll(edge, 12 + 32 * pair, 1),
                    pltpu.roll(edge, (20 + 32 * pair) % 128, 1),
                )
                total = one if total is None else jnp.where(lane // 32 == pair, one, total)
            merged[q, pl.ds(at, 16), :] = total.astype(BF16)
        return carry

    lax.fori_loop(0, 8, merge, 0)

    sub = iota((8, 128), 0)
    for end in range(2):
        at = 0 if end == 0 else 120
        mine = sub < 4 if end == 0 else sub >= 4
        for pair in range(4):
            for t in range(4):
                base = (pair * 4 + t) * 3
                for k, (one, two) in enumerate(((0, 1), (2, 3), (4, None))):
                    tile = source(one, pair, t, at, 8)
                    if two is not None:
                        tile = jnp.where(mine, tile, pltpu.roll(source(two, pair, t, at, 8), 4, 0))
                    vert_send[end, base + k] = tile.astype(BF16)
        for q in range(5):
            tile = merged[q, pl.ds(0 if end == 0 else 112, 16), :].astype(F32)
            tile = tile[0:8] if end == 0 else tile[8:16]
            vert_send[end, 48 + q] = tile.astype(BF16)

    for which in range(2):
        for pair in range(4):
            for t in range(4):
                rs[which, pair, t, 8:16, :] = st[which, pair, t, 128:136, :]
                rs[which, pair, t, 24:32, :] = st[which, pair, t, 8:16, :]

    pl.semaphore_wait(barrier, 8 + nrow - 1)

    def send(slot, src, dst, a, b):
        copy = pltpu.make_async_remote_copy(
            src_ref=src,
            dst_ref=dst,
            send_sem=send_sem.at[slot],
            recv_sem=recv_sem.at[slot],
            device_id=(a, b, row),
            device_id_type=MESH,
        )
        copy.start()
        return copy

    copies = [
        send(2, vert_send.at[1], vert.at[0], down, gy),
        send(3, vert_send.at[0], vert.at[1], up, gy),
        send(0, merged.at[pl.ds(0, 5)], side.at[0], gx, right),
        send(1, merged.at[pl.ds(0, 5)], side.at[1], gx, left),
        send(4, vert_send.at[1, pl.ds(48, 5)], diag.at[0], down, right),
        send(5, vert_send.at[1, pl.ds(48, 5)], diag.at[1], down, left),
        send(6, vert_send.at[0, pl.ds(48, 5)], diag.at[2], up, right),
        send(7, vert_send.at[0, pl.ds(48, 5)], diag.at[3], up, left),
    ]

    lane = iota((8, 128), 1)
    first_lane, last_lane = lane == 0, lane == 127

    def update_rows(array, s, at, u_of):
        x, y = s % 2, 1 - s % 2
        totals = [None] * 4
        for pair in range(4):
            centre = [array[y, pair, t, pl.ds(at, 8), :] for t in range(4)]
            on = [pltpu.roll(v, 1, 1) for v in centre]
            back = [pltpu.roll(v, 127, 1) for v in centre]
            for t in range(4):
                total = (
                    array[y, pair, t, pl.ds(at - 1, 8), :]
                    + array[y, pair, t, pl.ds(at + 1, 8), :]
                    + jnp.where(first_lane, on[(t + 3) % 4], on[t])
                    + jnp.where(last_lane, back[(t + 1) % 4], back[t])
                )
                value = new_value(array[x, pair, t, pl.ds(at, 8), :], total, u_of(pair, t))
                array[x, pair, t, pl.ds(at, 8), :] = value
                totals[t] = value if totals[t] is None else totals[t] + value
        return totals

    for s in range(4):

        def interior(c, carry, s=s):
            at = pl.multiple_of(c * 8, 8)
            totals = update_rows(st, s, 8 + at, lambda pair, t: uu[s, pair, t, pl.ds(at, 8), :])
            for t in range(4):
                sums[s, pl.ds(at, 8), 128 * t : 128 * t + 128] = totals[t]
            return carry

        lax.fori_loop(0, 16, interior, 0)

    for copy in copies:
        copy.wait()

    low = sub < 4
    for pair in range(4):
        for t in range(4):
            base = (pair * 4 + t) * 3
            for k in range(3):
                above = vert[0, base + k].astype(F32)
                below = vert[1, base + k].astype(F32)
                one = jnp.where(low, below, above)
                two = pltpu.roll(jnp.where(low, above, below), 4, 0)
                if k == 0:
                    rs[0, pair, t, 16:24, :] = one * SCALE
                    rs[1, pair, t, 16:24, :] = two * SCALE
                elif k == 1:
                    ub[0, pair, t] = one
                    ub[1, pair, t] = two
                else:
                    ub[2, pair, t] = one
    for s in range(4):
        for part in range(3):
            if s == 3 and part == 1:
                continue
            u_of = (
                lambda pair, t: uu[s, pair, t, 120:128, :],
                lambda pair, t: ub[s, pair, t],
                lambda pair, t: uu[s, pair, t, 0:8, :],
            )[part]
            totals = update_rows(rs, s, 8 + 8 * part, u_of)
            if part != 1:
                for t in range(4):
                    rsums[s, part // 2, :, 128 * t : 128 * t + 128] = totals[t]

    def strip(q, rows, own, from_left, from_right):
        _, small, even = lanes(rows)
        real0 = even if q % 2 == 0 else jnp.logical_not(even)
        take_left = jnp.logical_and(
            jnp.logical_or(small > 15, jnp.logical_and(small == 15, jnp.logical_not(real0))),
            jnp.logical_or(small < 19, jnp.logical_and(small == 19, real0)),
        )
        take_right = jnp.logical_and(
            jnp.logical_or(small > 11, jnp.logical_and(small == 11, jnp.logical_not(real0))),
            jnp.logical_or(small < 15, jnp.logical_and(small == 15, real0)),
        )
        return jnp.where(take_left, from_left, jnp.where(take_right, from_right, own))

    def put(q, at, rows, value):
        if q < 2:
            cs[q, pl.ds(8 + at, rows), :] = value * SCALE
        else:
            ucs[q - 2, pl.ds(at, rows), :] = value

    def strip_rows(c, carry):
        at = pl.multiple_of(c * 16, 16)
        for q in range(6):
            own = merged[q, pl.ds(at, 16), :].astype(F32)
            if q < 5:
                own = strip(
                    q,
                    16,
                    own,
                    side[0, q, pl.ds(at, 16), :].astype(F32),
                    side[1, q, pl.ds(at, 16), :].astype(F32),
                )
            put(q, 8 + at, 16, own)
        return carry

    lax.fori_loop(0, 8, strip_rows, 0)
    for end in range(2):
        for q in range(5):
            put(
                q,
                0 if end == 0 else 136,
                8,
                strip(
                    q,
                    8,
                    vert[end, 48 + q].astype(F32),
                    diag[2 * end, q].astype(F32),
                    diag[2 * end + 1, q].astype(F32),
                ),
            )
        ucs[3, (0 if end == 0 else 136) : (8 if end == 0 else 144), :] = zeros8

    column = iota((512, 128), 0)
    coarse = iota((512, 128), 1)
    inner = jnp.logical_and(coarse > 0, coarse < 127)
    pick0 = jnp.where(jnp.logical_and(inner, column // BLOCK == coarse), 1.0, 0.0).astype(BF16)
    pick1 = jnp.where(jnp.logical_and(inner, (column + 1) // BLOCK == coarse), 1.0, 0.0).astype(BF16)
    small = iota((128, 128), 0) % 32
    cell = iota((128, 128), 1)

    def strip_pick(shift):
        a = jnp.logical_and(cell == 127, jnp.logical_and(small >= 8 - shift, small < 12 - shift))
        b = jnp.logical_and(cell == 0, jnp.logical_and(small >= 20 - shift, small < 24 - shift))
        return jnp.where(jnp.logical_or(a, b), 1.0, 0.0).astype(BF16)

    edge0, edge1 = strip_pick(0), strip_pick(1)
    rows4 = jnp.where(iota((32, 128), 1) // BLOCK == iota((32, 128), 0), 1.0, 0.0).astype(BF16)
    tile_even = ((iota((128, 512), 0) + iota((128, 512), 1)) % 2) == 0
    strip_even = tile_even[:, 0:128]
    low_wide = iota((8, 512), 0) < 4

    def restricted(p, q):
        def whole(s):
            top = jnp.where(low_wide, rsums[s, 1], sums[s, 0:8, :])
            bottom = jnp.where(low_wide, sums[s, 120:128, :], rsums[s, 0])
            return jnp.concatenate([top, sums[s, 8:120, :], bottom], axis=0)

        even, odd = whole(p), whole(q)
        real0 = jnp.where(tile_even, even, odd)
        real1 = jnp.where(tile_even, odd, even)
        even, odd = cs[0, 16:144, :], cs[1, 16:144, :]
        strip0 = jnp.where(strip_even, even, odd)
        strip1 = jnp.where(strip_even, odd, even)
        by_column = (
            split_dot(real0, pick0)
            + split_dot(real1, pick1)
            + split_dot(strip0, edge0)
            + split_dot(strip1, edge1)
        )
        return split_dot_left(rows4, by_column)

    def share(which):
        out = []
        for d in range(1, nrow):
            copy = pltpu.make_async_remote_copy(
                src_ref=red_send.at[which],
                dst_ref=red.at[d - 1, which],
                send_sem=red_send_sem.at[which, d - 1],
                recv_sem=red_recv_sem.at[which, d - 1],
                device_id=(gx, gy, peers[d - 1]),
                device_id_type=MESH,
            )
            copy.start()
            out.append(copy)
        return out

    shared = []
    for s in range(4):
        x, y = s % 2, 1 - s % 2

        def strip_sweep(c, carry, s=s, x=x, y=y):
            at = pl.multiple_of(c * 8, 8)
            centre = cs[y, pl.ds(8 + at, 8), :]
            total = (
                cs[y, pl.ds(7 + at, 8), :]
                + cs[y, pl.ds(9 + at, 8), :]
                + pltpu.roll(centre, 1, 1)
                + pltpu.roll(centre, 127, 1)
            )
            cs[x, pl.ds(8 + at, 8), :] = new_value(
                cs[x, pl.ds(8 + at, 8), :], total, ucs[s, pl.ds(at, 8), :]
            )
            return carry

        lax.fori_loop(0, 18, strip_sweep, 0, unroll=3)
        if s % 2 == 1:
            red_send[s // 2] = restricted(s - 1, s)
            shared += share(s // 2)

    for copy in shared:
        copy.wait()
    averages = []
    for which in range(2):
        total = red_send[which]
        for d in range(1, nrow):
            total = total + red[d - 1, which]
        averages.append(total * (1.0 / (SCALE * 8 * nrow * BLOCK * BLOCK)))
    cov_ref[...] = averages[1]
    proj_ref[...] = averages[1] + (LEAP / 2.0) * (averages[1] - averages[0])


def solution(mesh):
    sizes = tuple(mesh.shape[a] for a in ("gx", "gy", "row"))
    nrow = sizes[2]

    def per_device(occupancy, random_draws):
        any_space = pl.BlockSpec(memory_space=pl.ANY)
        vmem = pl.BlockSpec(memory_space=pltpu.VMEM)
        return pl.pallas_call(
            functools.partial(kernel, sizes),
            name="burst",
            out_shape=[jax.ShapeDtypeStruct((32, 128), F32)] * 2,
            in_specs=[any_space, any_space],
            out_specs=[vmem, vmem],
            scratch_shapes=[
                pltpu.VMEM((8, 128, 512), jnp.int32),
                pltpu.VMEM((4, 8, 128, 512), BF16),
                pltpu.VMEM((2, 4, 4, 144, 128), F32),
                pltpu.VMEM((4, 4, 4, 128, 128), F32),
                pltpu.VMEM((4, 128, 512), F32),
                pltpu.VMEM((2, 4, 4, 40, 128), F32),
                pltpu.VMEM((3, 4, 4, 8, 128), F32),
                pltpu.VMEM((4, 2, 8, 512), F32),
                pltpu.VMEM((2, 160, 128), F32),
                pltpu.VMEM((4, 144, 128), F32),
                pltpu.VMEM((6, 128, 128), BF16),
                pltpu.VMEM((2, 5, 128, 128), BF16),
                pltpu.VMEM((2, 53, 8, 128), BF16),
                pltpu.VMEM((2, 53, 8, 128), BF16),
                pltpu.VMEM((4, 5, 8, 128), BF16),
                pltpu.VMEM((2, 32, 128), F32),
                pltpu.VMEM((nrow - 1, 2, 32, 128), F32),
                pltpu.SemaphoreType.DMA((2, 4)),
                pltpu.SemaphoreType.DMA((8,)),
                pltpu.SemaphoreType.DMA((8,)),
                pltpu.SemaphoreType.DMA((2, nrow - 1)),
                pltpu.SemaphoreType.DMA((2, nrow - 1)),
            ],
            compiler_params=pltpu.CompilerParams(
                collective_id=0, has_side_effects=True, vmem_limit_bytes=48 * 1024 * 1024
            ),
        )(occupancy, random_draws)

    return jax.shard_map(
        per_device,
        mesh=mesh,
        in_specs=(P("row", "gx", "gy"), P(None, "row", "gx", "gy")),
        out_specs=(P("gx", "gy"), P("gx", "gy")),
        check_vma=False,
    )
```

```python
import functools

import jax
import jax.numpy as jnp
import numpy as np
from jax import lax
from jax.experimental import pallas as pl
from jax.experimental.pallas import tpu as pltpu
from jax.sharding import PartitionSpec as P

MESH = pl.DeviceIdType.MESH
BLOCK = 4
LEAP = 8
SCALE = float(-0.5 * np.log2(np.e))
F32 = jnp.float32
BF16 = jnp.bfloat16


def iota(shape, dim):
    return lax.broadcasted_iota(jnp.int32, shape, dim)


def new_value(x, total, u):
    gone = 0.6 - 0.6 * jnp.exp2(total)
    kept = x * gone
    return (0.1 * x + kept) + u * (0.6 * SCALE - kept) + 0.075 * total


def split_dot(x, onehot):
    high = x.astype(BF16)
    low = (x - high.astype(F32)).astype(BF16)
    return jnp.dot(high, onehot, preferred_element_type=F32) + jnp.dot(
        low, onehot, preferred_element_type=F32
    )


def split_dot_left(onehot, x):
    high = x.astype(BF16)
    low = (x - high.astype(F32)).astype(BF16)
    return jnp.dot(onehot, high, preferred_element_type=F32) + jnp.dot(
        onehot, low, preferred_element_type=F32
    )


def kernel(
    sizes,
    occ_hbm,
    u_hbm,
    average_ref,
    occ,
    draws,
    st,
    uu,
    sums,
    rs,
    ub,
    rsums,
    cs,
    ucs,
    merged,
    side,
    vert_send,
    vert,
    diag,
    red_send,
    red,
    load_sem,
    send_sem,
    recv_sem,
    red_send_sem,
    red_recv_sem,
):
    ngx, ngy, nrow = sizes
    gx, gy, row = lax.axis_index("gx"), lax.axis_index("gy"), lax.axis_index("row")
    up, down = lax.rem(gx + ngx - 1, ngx), lax.rem(gx + 1, ngx)
    left, right = lax.rem(gy + ngy - 1, ngy), lax.rem(gy + 1, ngy)

    def load(pair):
        return (
            pltpu.make_async_copy(
                occ_hbm.at[pl.ds(2 * pair, 2)], occ.at[pl.ds(2 * pair, 2)], load_sem.at[0, pair]
            ),
            pltpu.make_async_copy(
                u_hbm.at[:, pl.ds(2 * pair, 2)],
                draws.at[:, pl.ds(2 * pair, 2)],
                load_sem.at[1, pair],
            ),
        )

    for pair in range(4):
        for copy in load(pair):
            copy.start()

    barrier = pltpu.get_barrier_semaphore()
    lattice = [
        (gx, left),
        (gx, right),
        (up, gy),
        (down, gy),
        (up, left),
        (up, right),
        (down, left),
        (down, right),
    ]
    for a, b in lattice:
        pl.semaphore_signal(barrier, inc=1, device_id=(a, b, row), device_id_type=MESH)
    peers = [lax.rem(row + d, nrow) for d in range(1, nrow)]
    for peer in peers:
        pl.semaphore_signal(barrier, inc=1, device_id=(gx, gy, peer), device_id_type=MESH)

    zeros8 = jnp.zeros((8, 128), F32)
    for which in range(2):
        for pair in range(4):
            for t in range(4):
                st[which, pair, t, 0:8, :] = zeros8
                st[which, pair, t, 136:144, :] = zeros8
                rs[which, pair, t, 0:8, :] = zeros8
                rs[which, pair, t, 32:40, :] = zeros8
        cs[which, 0:8, :] = zeros8
        cs[which, 152:160, :] = zeros8

    wide_even = ((iota((16, 512), 0) + iota((16, 512), 1)) % 2) == 0
    for pair in range(4):
        for copy in load(pair):
            copy.wait()

        def pack(c, carry, pair=pair):
            at = pl.multiple_of(c * 16, 16)
            first = occ[2 * pair, pl.ds(at, 16), :].astype(F32) * SCALE
            second = pltpu.roll(occ[2 * pair + 1, pl.ds(at, 16), :].astype(F32) * SCALE, 511, 1)
            both = (
                jnp.where(wide_even, first, second),
                jnp.where(wide_even, second, first),
            )
            for which in range(2):
                for t in range(4):
                    st[which, pair, t, pl.ds(8 + at, 16), :] = both[which][:, 128 * t : 128 * t + 128]
            for s in range(4):
                first = draws[s, 2 * pair, pl.ds(at, 16), :].astype(F32)
                second = pltpu.roll(draws[s, 2 * pair + 1, pl.ds(at, 16), :].astype(F32), 511, 1)
                chosen = (
                    jnp.where(wide_even, first, second)
                    if s % 2 == 0
                    else jnp.where(wide_even, second, first)
                )
                for t in range(4):
                    uu[s, pair, t, pl.ds(at, 16), :] = chosen[:, 128 * t : 128 * t + 128]
            return carry

        lax.fori_loop(0, 8, pack, 0, unroll=4)

    def source(q, pair, t, at, size):
        if q < 2:
            return st[q, pair, t, pl.ds(8 + at, size), :] * (1.0 / SCALE)
        return uu[q - 2, pair, t, pl.ds(at, size), :]

    def lanes(rows):
        lane = iota((rows, 128), 1)
        even = ((iota((rows, 128), 0) + lane) % 2) == 0
        return lane, lane % 32, even

    def merge(c, carry):
        at = pl.multiple_of(c * 16, 16)
        lane, small, even = lanes(16)
        for q in range(6):
            real0 = even if q % 2 == 0 else jnp.logical_not(even)
            early = jnp.logical_or(small < 15, jnp.logical_and(small == 15, real0))
            total = None
            for pair in range(4):
                edge = jnp.where(lane >= 64, source(q, pair, 3, at, 16), source(q, pair, 0, at, 16))
                one = jnp.where(
                    early,
                    pltpu.roll(edge, 12 + 32 * pair, 1),
                    pltpu.roll(edge, (20 + 32 * pair) % 128, 1),
                )
                total = one if total is None else jnp.where(lane // 32 == pair, one, total)
            merged[q, pl.ds(at, 16), :] = total.astype(BF16)
        return carry

    lax.fori_loop(0, 8, merge, 0, unroll=2)

    sub = iota((8, 128), 0)
    for end in range(2):
        at = 0 if end == 0 else 120
        mine = sub < 4 if end == 0 else sub >= 4
        for pair in range(4):
            for t in range(4):
                base = (pair * 4 + t) * 3
                for k, (one, two) in enumerate(((0, 1), (2, 3), (4, None))):
                    tile = source(one, pair, t, at, 8)
                    if two is not None:
                        tile = jnp.where(mine, tile, pltpu.roll(source(two, pair, t, at, 8), 4, 0))
                    vert_send[end, base + k] = tile.astype(BF16)
        for q in range(5):
            tile = merged[q, pl.ds(0 if end == 0 else 112, 16), :].astype(F32)
            tile = tile[0:8] if end == 0 else tile[8:16]
            vert_send[end, 48 + q] = tile.astype(BF16)

    for which in range(2):
        for pair in range(4):
            for t in range(4):
                rs[which, pair, t, 8:16, :] = st[which, pair, t, 128:136, :]
                rs[which, pair, t, 24:32, :] = st[which, pair, t, 8:16, :]

    pl.semaphore_wait(barrier, 8 + nrow - 1)

    def send(slot, src, dst, a, b):
        copy = pltpu.make_async_remote_copy(
            src_ref=src,
            dst_ref=dst,
            send_sem=send_sem.at[slot],
            recv_sem=recv_sem.at[slot],
            device_id=(a, b, row),
            device_id_type=MESH,
        )
        copy.start()
        return copy

    copies = [
        send(2, vert_send.at[1], vert.at[0], down, gy),
        send(3, vert_send.at[0], vert.at[1], up, gy),
        send(0, merged.at[pl.ds(0, 5)], side.at[0], gx, right),
        send(1, merged.at[pl.ds(0, 5)], side.at[1], gx, left),
        send(4, vert_send.at[1, pl.ds(48, 5)], diag.at[0], down, right),
        send(5, vert_send.at[1, pl.ds(48, 5)], diag.at[1], down, left),
        send(6, vert_send.at[0, pl.ds(48, 5)], diag.at[2], up, right),
        send(7, vert_send.at[0, pl.ds(48, 5)], diag.at[3], up, left),
    ]

    lane = iota((8, 128), 1)
    first_lane, last_lane = lane == 0, lane == 127

    def update_rows(array, s, at, u_of):
        x, y = s % 2, 1 - s % 2
        totals = [None] * 4
        for pair in range(4):
            centre = [array[y, pair, t, pl.ds(at, 8), :] for t in range(4)]
            on = [pltpu.roll(v, 1, 1) for v in centre]
            back = [pltpu.roll(v, 127, 1) for v in centre]
            for t in range(4):
                total = (
                    array[y, pair, t, pl.ds(at - 1, 8), :]
                    + array[y, pair, t, pl.ds(at + 1, 8), :]
                    + jnp.where(first_lane, on[(t + 3) % 4], on[t])
                    + jnp.where(last_lane, back[(t + 1) % 4], back[t])
                )
                value = new_value(array[x, pair, t, pl.ds(at, 8), :], total, u_of(pair, t))
                array[x, pair, t, pl.ds(at, 8), :] = value
                totals[t] = value if totals[t] is None else totals[t] + value
        return totals

    for s in range(4):

        def interior(c, carry, s=s):
            at = pl.multiple_of(c * 8, 8)
            totals = update_rows(st, s, 8 + at, lambda pair, t: uu[s, pair, t, pl.ds(at, 8), :])
            for t in range(4):
                sums[s, pl.ds(at, 8), 128 * t : 128 * t + 128] = totals[t]
            return carry

        lax.fori_loop(0, 16, interior, 0, unroll=16)

    for copy in copies:
        copy.wait()

    low = sub < 4
    for pair in range(4):
        for t in range(4):
            base = (pair * 4 + t) * 3
            for k in range(3):
                above = vert[0, base + k].astype(F32)
                below = vert[1, base + k].astype(F32)
                one = jnp.where(low, below, above)
                two = pltpu.roll(jnp.where(low, above, below), 4, 0)
                if k == 0:
                    rs[0, pair, t, 16:24, :] = one * SCALE
                    rs[1, pair, t, 16:24, :] = two * SCALE
                elif k == 1:
                    ub[0, pair, t] = one
                    ub[1, pair, t] = two
                else:
                    ub[2, pair, t] = one
    for s in range(4):
        for part in range(3):
            if s == 3 and part == 1:
                continue
            u_of = (
                lambda pair, t: uu[s, pair, t, 120:128, :],
                lambda pair, t: ub[s, pair, t],
                lambda pair, t: uu[s, pair, t, 0:8, :],
            )[part]
            totals = update_rows(rs, s, 8 + 8 * part, u_of)
            if part != 1:
                for t in range(4):
                    rsums[s, part // 2, :, 128 * t : 128 * t + 128] = totals[t]

    def strip(q, rows, own, from_left, from_right):
        _, small, even = lanes(rows)
        real0 = even if q % 2 == 0 else jnp.logical_not(even)
        take_left = jnp.logical_and(
            jnp.logical_or(small > 15, jnp.logical_and(small == 15, jnp.logical_not(real0))),
            jnp.logical_or(small < 19, jnp.logical_and(small == 19, real0)),
        )
        take_right = jnp.logical_and(
            jnp.logical_or(small > 11, jnp.logical_and(small == 11, jnp.logical_not(real0))),
            jnp.logical_or(small < 15, jnp.logical_and(small == 15, real0)),
        )
        return jnp.where(take_left, from_left, jnp.where(take_right, from_right, own))

    def put(q, at, rows, value):
        if q < 2:
            cs[q, pl.ds(8 + at, rows), :] = value * SCALE
        else:
            ucs[q - 2, pl.ds(at, rows), :] = value

    def strip_rows(c, carry):
        at = pl.multiple_of(c * 16, 16)
        for q in range(6):
            own = merged[q, pl.ds(at, 16), :].astype(F32)
            if q < 5:
                own = strip(
                    q,
                    16,
                    own,
                    side[0, q, pl.ds(at, 16), :].astype(F32),
                    side[1, q, pl.ds(at, 16), :].astype(F32),
                )
            put(q, 8 + at, 16, own)
        return carry

    lax.fori_loop(0, 8, strip_rows, 0, unroll=2)
    for end in range(2):
        for q in range(5):
            put(
                q,
                0 if end == 0 else 136,
                8,
                strip(
                    q,
                    8,
                    vert[end, 48 + q].astype(F32),
                    diag[2 * end, q].astype(F32),
                    diag[2 * end + 1, q].astype(F32),
                ),
            )
        ucs[3, (0 if end == 0 else 136) : (8 if end == 0 else 144), :] = zeros8

    column = iota((512, 128), 0)
    coarse = iota((512, 128), 1)
    inner = jnp.logical_and(coarse > 0, coarse < 127)
    pick0 = jnp.where(jnp.logical_and(inner, column // BLOCK == coarse), 1.0, 0.0).astype(BF16)
    pick1 = jnp.where(jnp.logical_and(inner, (column + 1) // BLOCK == coarse), 1.0, 0.0).astype(BF16)
    small = iota((128, 128), 0) % 32
    cell = iota((128, 128), 1)

    def strip_pick(shift):
        a = jnp.logical_and(cell == 127, jnp.logical_and(small >= 8 - shift, small < 12 - shift))
        b = jnp.logical_and(cell == 0, jnp.logical_and(small >= 20 - shift, small < 24 - shift))
        return jnp.where(jnp.logical_or(a, b), 1.0, 0.0).astype(BF16)

    edge0, edge1 = strip_pick(0), strip_pick(1)
    rows4 = jnp.where(iota((32, 128), 1) // BLOCK == iota((32, 128), 0), 1.0, 0.0).astype(BF16)
    tile_even = ((iota((128, 512), 0) + iota((128, 512), 1)) % 2) == 0
    strip_even = tile_even[:, 0:128]
    low_wide = iota((8, 512), 0) < 4

    def restricted(p, q):
        def whole(s):
            top = jnp.where(low_wide, rsums[s, 1], sums[s, 0:8, :])
            bottom = jnp.where(low_wide, sums[s, 120:128, :], rsums[s, 0])
            return jnp.concatenate([top, sums[s, 8:120, :], bottom], axis=0)

        even, odd = whole(p), whole(q)
        real0 = jnp.where(tile_even, even, odd)
        real1 = jnp.where(tile_even, odd, even)
        even, odd = cs[0, 16:144, :], cs[1, 16:144, :]
        strip0 = jnp.where(strip_even, even, odd)
        strip1 = jnp.where(strip_even, odd, even)
        by_column = (
            split_dot(real0, pick0)
            + split_dot(real1, pick1)
            + split_dot(strip0, edge0)
            + split_dot(strip1, edge1)
        )
        return split_dot_left(rows4, by_column)

    def share(which):
        out = []
        for d in range(1, nrow):
            copy = pltpu.make_async_remote_copy(
                src_ref=red_send.at[which],
                dst_ref=red.at[d - 1, which],
                send_sem=red_send_sem.at[which, d - 1],
                recv_sem=red_recv_sem.at[which, d - 1],
                device_id=(gx, gy, peers[d - 1]),
                device_id_type=MESH,
            )
            copy.start()
            out.append(copy)
        return out

    shared = []
    for s in range(4):
        x, y = s % 2, 1 - s % 2

        def strip_sweep(c, carry, s=s, x=x, y=y):
            at = pl.multiple_of(c * 8, 8)
            centre = cs[y, pl.ds(8 + at, 8), :]
            total = (
                cs[y, pl.ds(7 + at, 8), :]
                + cs[y, pl.ds(9 + at, 8), :]
                + pltpu.roll(centre, 1, 1)
                + pltpu.roll(centre, 127, 1)
            )
            cs[x, pl.ds(8 + at, 8), :] = new_value(
                cs[x, pl.ds(8 + at, 8), :], total, ucs[s, pl.ds(at, 8), :]
            )
            return carry

        lax.fori_loop(0, 18, strip_sweep, 0, unroll=18)
        if s % 2 == 1:
            red_send[s // 2] = restricted(s - 1, s)
            shared += share(s // 2)

    for copy in shared:
        copy.wait()
    for which in range(2):
        total = red_send[which]
        for d in range(1, nrow):
            total = total + red[d - 1, which]
        average_ref[which] = total * (1.0 / (SCALE * 8 * nrow * BLOCK * BLOCK))


def solution(mesh):
    sizes = tuple(mesh.shape[a] for a in ("gx", "gy", "row"))
    nrow = sizes[2]

    def per_device(occupancy, random_draws):
        any_space = pl.BlockSpec(memory_space=pl.ANY)
        vmem = pl.BlockSpec(memory_space=pltpu.VMEM)
        averages = pl.pallas_call(
            functools.partial(kernel, sizes),
            name="burst",
            out_shape=jax.ShapeDtypeStruct((2, 32, 128), F32),
            in_specs=[any_space, any_space],
            out_specs=vmem,
            scratch_shapes=[
                pltpu.VMEM((8, 128, 512), jnp.int32),
                pltpu.VMEM((4, 8, 128, 512), BF16),
                pltpu.VMEM((2, 4, 4, 144, 128), F32),
                pltpu.VMEM((4, 4, 4, 128, 128), F32),
                pltpu.VMEM((4, 128, 512), F32),
                pltpu.VMEM((2, 4, 4, 40, 128), F32),
                pltpu.VMEM((3, 4, 4, 8, 128), F32),
                pltpu.VMEM((4, 2, 8, 512), F32),
                pltpu.VMEM((2, 160, 128), F32),
                pltpu.VMEM((4, 144, 128), F32),
                pltpu.VMEM((6, 128, 128), BF16),
                pltpu.VMEM((2, 5, 128, 128), BF16),
                pltpu.VMEM((2, 53, 8, 128), BF16),
                pltpu.VMEM((2, 53, 8, 128), BF16),
                pltpu.VMEM((4, 5, 8, 128), BF16),
                pltpu.VMEM((2, 32, 128), F32),
                pltpu.VMEM((nrow - 1, 2, 32, 128), F32),
                pltpu.SemaphoreType.DMA((2, 4)),
                pltpu.SemaphoreType.DMA((8,)),
                pltpu.SemaphoreType.DMA((8,)),
                pltpu.SemaphoreType.DMA((2, nrow - 1)),
                pltpu.SemaphoreType.DMA((2, nrow - 1)),
            ],
            compiler_params=pltpu.CompilerParams(
                collective_id=0, has_side_effects=True, vmem_limit_bytes=62 * 1024 * 1024
            ),
        )(occupancy, random_draws)
        coverage = averages[1]
        return coverage, coverage + (LEAP / 2.0) * (coverage - averages[0])

    return jax.shard_map(
        per_device,
        mesh=mesh,
        in_specs=(P("row", "gx", "gy"), P(None, "row", "gx", "gy")),
        out_specs=(P("gx", "gy"), P("gx", "gy")),
        check_vma=False,
    )
```

```python
import functools

import jax
import jax.numpy as jnp
import numpy as np
from jax import lax
from jax.experimental import pallas as pl
from jax.experimental.pallas import tpu as pltpu
from jax.sharding import PartitionSpec as P

MESH = pl.DeviceIdType.MESH
BLOCK = 4
LEAP = 8
SCALE = float(-0.5 * np.log2(np.e))
F32 = jnp.float32
BF16 = jnp.bfloat16


def iota(shape, dim):
    return lax.broadcasted_iota(jnp.int32, shape, dim)


def new_value(x, total, u):
    gone = 0.6 - 0.6 * jnp.exp2(total)
    kept = x * gone
    return (0.1 * x + kept) + u * (0.6 * SCALE - kept) + 0.075 * total


def split_dot(x, onehot):
    high = x.astype(BF16)
    low = (x - high.astype(F32)).astype(BF16)
    return jnp.dot(high, onehot, preferred_element_type=F32) + jnp.dot(
        low, onehot, preferred_element_type=F32
    )


def split_dot_left(onehot, x):
    high = x.astype(BF16)
    low = (x - high.astype(F32)).astype(BF16)
    return jnp.dot(onehot, high, preferred_element_type=F32) + jnp.dot(
        onehot, low, preferred_element_type=F32
    )


def kernel(
    sizes,
    occ_hbm,
    u_hbm,
    average_ref,
    occ,
    draws,
    st,
    uu,
    sums,
    rs,
    ub,
    rsums,
    cs,
    ucs,
    place,
    pick,
    edge_pick,
    merged,
    side_send,
    side,
    corner_send,
    corner,
    vert_send,
    vert,
    main_part,
    red_send,
    red,
    load_sem,
    send_sem,
    recv_sem,
    red_send_sem,
    red_recv_sem,
):
    ngx, ngy, nrow = sizes
    gx, gy, row = lax.axis_index("gx"), lax.axis_index("gy"), lax.axis_index("row")
    up, down = lax.rem(gx + ngx - 1, ngx), lax.rem(gx + 1, ngx)
    left, right = lax.rem(gy + ngy - 1, ngy), lax.rem(gy + 1, ngy)

    loads = []

    def load(group, src, dst):
        copy = pltpu.make_async_copy(src, dst, load_sem.at[len(loads)])
        copy.start()
        loads.append((group, copy))

    def arrived(group):
        for which, copy in loads:
            if which == group:
                copy.wait()

    def load_occ(group, reals, rows, columns):
        at = (pl.ds(*reals), pl.ds(*rows), pl.ds(*columns))
        load(group, occ_hbm.at[at], occ.at[at])

    def load_u(group, sweeps, reals, rows, columns):
        at = (pl.ds(*sweeps), pl.ds(*reals), pl.ds(*rows), pl.ds(*columns))
        load(group, u_hbm.at[at], draws.at[at])

    load_occ("pair0", (0, 2), (0, 128), (0, 512))
    load_u("pair0", (0, 4), (0, 2), (0, 128), (0, 512))
    for columns in ((0, 128), (384, 128)):
        load_occ("edges", (2, 6), (0, 128), columns)
        load_u("edges", (0, 4), (2, 6), (0, 128), columns)
    for rows in ((0, 16), (112, 16)):
        load_occ("edges", (2, 6), rows, (128, 256))
        load_u("edges", (0, 3), (2, 6), rows, (128, 256))
    for pair in range(1, 4):
        load_occ("pair%d" % pair, (2 * pair, 2), (16, 96), (128, 256))
        load_u("pair%d" % pair, (0, 3), (2 * pair, 2), (16, 96), (128, 256))
        load_u("pair%d" % pair, (3, 1), (2 * pair, 2), (0, 128), (128, 256))

    barrier = pltpu.get_barrier_semaphore()
    lattice = [
        (gx, left),
        (gx, right),
        (up, gy),
        (down, gy),
        (up, left),
        (up, right),
        (down, left),
        (down, right),
    ]
    for a, b in lattice:
        pl.semaphore_signal(barrier, inc=1, device_id=(a, b, row), device_id_type=MESH)
    peers = [lax.rem(row + d, nrow) for d in range(1, nrow)]
    for peer in peers:
        pl.semaphore_signal(barrier, inc=1, device_id=(gx, gy, peer), device_id_type=MESH)

    zeros8 = jnp.zeros((8, 128), F32)
    for which in range(2):
        for pair in range(4):
            for t in range(4):
                st[which, pair, t, 0:8, :] = zeros8
                st[which, pair, t, 136:144, :] = zeros8
                rs[which, pair, t, 0:8, :] = zeros8
                rs[which, pair, t, 32:40, :] = zeros8
        cs[which, 0:8, :] = zeros8
        cs[which, 152:160, :] = zeros8
    ucs[3, 0:8, :] = zeros8
    ucs[3, 136:144, :] = zeros8

    k = iota((256, 128), 0)
    far = k - 128
    for real in range(2):
        for pair in range(4):
            to = iota((256, 128), 1) - 32 * pair + real
            hit = ((k < 4) & (to == k + 12)) | ((k < 8) & (to == k + 20))
            hit |= ((far >= 120) & (to == far - 116)) | ((far >= 124) & (to == far - 108))
            place[real, 256 * pair : 256 * pair + 256, :] = jnp.where(hit, 1.0, 0.0).astype(BF16)
        column = iota((512, 128), 0) + real
        coarse = iota((512, 128), 1)
        hit = (coarse > 0) & (coarse < 127) & (column // BLOCK == coarse)
        pick[real] = jnp.where(hit, 1.0, 0.0).astype(BF16)
        small = iota((128, 128), 0) % 32 + real
        cell = iota((128, 128), 1)
        hit = ((cell == 127) & (small >= 8) & (small < 12)) | (
            (cell == 0) & (small >= 20) & (small < 24)
        )
        edge_pick[real] = jnp.where(hit, 1.0, 0.0).astype(BF16)

    sub = iota((8, 128), 0)
    low = sub < 4
    lane = iota((8, 128), 1)
    first_lane, last_lane = lane == 0, lane == 127
    wide_even = ((iota((16, 512), 0) + iota((16, 512), 1)) % 2) == 0
    tile_even = ((iota((128, 128), 0) + iota((128, 128), 1)) % 2) == 0

    def update_rows(array, s, at, pairs, u_of):
        x, y = s % 2, 1 - s % 2
        totals = [None] * 4
        for pair in pairs:
            centre = [array[y, pair, t, pl.ds(at, 8), :] for t in range(4)]
            on = [pltpu.roll(v, 1, 1) for v in centre]
            back = [pltpu.roll(v, 127, 1) for v in centre]
            for t in range(4):
                total = (
                    array[y, pair, t, pl.ds(at - 1, 8), :]
                    + array[y, pair, t, pl.ds(at + 1, 8), :]
                    + jnp.where(first_lane, on[(t + 3) % 4], on[t])
                    + jnp.where(last_lane, back[(t + 1) % 4], back[t])
                )
                value = new_value(array[x, pair, t, pl.ds(at, 8), :], total, u_of(pair, t))
                array[x, pair, t, pl.ds(at, 8), :] = value
                totals[t] = value if totals[t] is None else totals[t] + value
        return totals

    def paired(first, second, even, which):
        shifted = pltpu.roll(second, 511, 1)
        return jnp.where(even, first, shifted) if which == 0 else jnp.where(even, shifted, first)

    def pack(pair):
        def rows(c, carry):
            at = pl.multiple_of(c * 16, 16)
            first = occ[2 * pair, pl.ds(at, 16), :].astype(F32) * SCALE
            second = occ[2 * pair + 1, pl.ds(at, 16), :].astype(F32) * SCALE
            for which in range(2):
                both = paired(first, second, wide_even, which)
                for t in range(4):
                    st[which, pair, t, pl.ds(8 + at, 16), :] = both[:, 128 * t : 128 * t + 128]
            for s in range(4):
                first = draws[s, 2 * pair, pl.ds(at, 16), :].astype(F32)
                second = draws[s, 2 * pair + 1, pl.ds(at, 16), :].astype(F32)
                both = paired(first, second, wide_even, s % 2)
                for t in range(4):
                    uu[s, pair, t, pl.ds(at, 16), :] = both[:, 128 * t : 128 * t + 128]
            return carry

        lax.fori_loop(0, 8, rows, 0, unroll=4)
        for which in range(2):
            for t in range(4):
                rs[which, pair, t, 8:16, :] = st[which, pair, t, 128:136, :]
                rs[which, pair, t, 24:32, :] = st[which, pair, t, 8:16, :]

    def interior(pair):
        for s in range(4):

            def rows(c, carry, s=s):
                at = pl.multiple_of(c * 8, 8)
                totals = update_rows(
                    st, s, 8 + at, (pair,), lambda p, t: uu[s, p, t, pl.ds(at, 8), :]
                )
                for t in range(4):
                    columns = slice(128 * t, 128 * t + 128)
                    if pair == 0:
                        sums[s, pl.ds(at, 8), columns] = totals[t]
                    else:
                        sums[s, pl.ds(at, 8), columns] += totals[t]
                return carry

            lax.fori_loop(0, 16, rows, 0, unroll=16)

    arrived("pair0")
    pack(0)
    interior(0)
    arrived("edges")

    def edge_columns(real, load_real):
        tiles = []
        for pair in range(4):
            tiles += [load_real(2 * pair + real, 0), load_real(2 * pair + real, 384)]
        return jnp.dot(
            jnp.concatenate(tiles, axis=1), place[real], preferred_element_type=F32
        )

    def put_merged(q, value):
        merged[q] = value.astype(BF16)
        return value

    wholes = [edge_columns(r, lambda i, c: occ[i, :, c : c + 128].astype(F32).astype(BF16)) for r in (0, 1)]
    strips = [
        put_merged(0, jnp.where(tile_even, wholes[0], wholes[1])),
        put_merged(1, jnp.where(tile_even, wholes[1], wholes[0])),
    ]
    for s in range(4):
        wholes = [edge_columns(r, lambda i, c: draws[s, i, :, c : c + 128]) for r in (0, 1)]
        strips.append(
            put_merged(2 + s, jnp.where(tile_even, wholes[s % 2], wholes[1 - s % 2]))
        )
    slot = (iota((128, 128), 1) % 32) // 9
    sent = (
        jnp.where(
            slot == 0,
            pltpu.roll(strips[0], 117, 1),
            jnp.where(slot == 1, pltpu.roll(strips[1], 126, 1), pltpu.roll(strips[2], 7, 1)),
        ),
        jnp.where(slot == 0, pltpu.roll(strips[3], 117, 1), pltpu.roll(strips[4], 126, 1)),
    )
    for part in range(2):
        side_send[part] = sent[part].astype(BF16)
        corner_send[0, part] = sent[part][0:8].astype(BF16)
        corner_send[1, part] = sent[part][120:128].astype(BF16)
    for q in range(5):
        vert_send[0, 32 + q] = strips[q][0:8].astype(BF16)
        vert_send[1, 32 + q] = strips[q][120:128].astype(BF16)

    even8 = wide_even[0:8]
    sub_wide = iota((8, 512), 0)
    for end in range(2):
        at = 0 if end == 0 else 112
        keep = slice(0, 8) if end == 0 else slice(8, 16)
        mine = sub_wide < 4 if end == 0 else sub_wide >= 4
        outer = sub_wide == (7 if end == 0 else 0)
        for pair in range(4):
            first = occ[2 * pair, at : at + 16, :][keep].astype(F32)
            second = occ[2 * pair + 1, at : at + 16, :][keep].astype(F32)
            p, q = paired(first, second, even8, 0), paired(first, second, even8, 1)
            u = [
                paired(
                    draws[s, 2 * pair, at : at + 16, :].astype(F32)[keep],
                    draws[s, 2 * pair + 1, at : at + 16, :].astype(F32)[keep],
                    even8,
                    s % 2,
                )
                for s in range(3)
            ]
            tiles = (
                jnp.where(
                    mine,
                    q,
                    jnp.where(outer, pltpu.roll(u[2], 7 if end == 0 else 1, 0), pltpu.roll(u[0], 4, 0)),
                ),
                jnp.where(mine, p, pltpu.roll(u[1], 4, 0)),
            )
            for n in range(2):
                packed = tiles[n].astype(BF16)
                for t in range(4):
                    vert_send[end, 8 * pair + 2 * t + n] = packed[:, 128 * t : 128 * t + 128]

    pl.semaphore_wait(barrier, 8 + nrow - 1)

    def send(slot, src, dst, a, b):
        copy = pltpu.make_async_remote_copy(
            src_ref=src,
            dst_ref=dst,
            send_sem=send_sem.at[slot],
            recv_sem=recv_sem.at[slot],
            device_id=(a, b, row),
            device_id_type=MESH,
        )
        copy.start()
        return copy

    copies = [
        send(4, corner_send.at[1], corner.at[0], down, right),
        send(5, corner_send.at[1], corner.at[1], down, left),
        send(6, corner_send.at[0], corner.at[2], up, right),
        send(7, corner_send.at[0], corner.at[3], up, left),
        send(2, vert_send.at[1], vert.at[0], down, gy),
        send(3, vert_send.at[0], vert.at[1], up, gy),
        send(0, side_send, side.at[0], gx, right),
        send(1, side_send, side.at[1], gx, left),
    ]

    for pair in range(1, 4):
        arrived("pair%d" % pair)
        pack(pair)
        interior(pair)

    coarse_row = iota((32, 128), 0)
    all_rows = iota((32, 128), 1) // BLOCK == coarse_row
    rows_all = jnp.where(all_rows, 1.0, 0.0).astype(BF16)
    rows_inner = jnp.where(all_rows & (coarse_row > 0) & (coarse_row < 31), 1.0, 0.0).astype(BF16)
    even_wide = ((iota((128, 512), 0) + iota((128, 512), 1)) % 2) == 0

    for which in range(2):
        p, q = sums[2 * which], sums[2 * which + 1]
        by_column = split_dot(jnp.where(even_wide, p, q), pick[0]) + split_dot(
            jnp.where(even_wide, q, p), pick[1]
        )
        main_part[which] = split_dot_left(rows_inner, by_column)

    for copy in copies:
        copy.wait()

    for pair in range(4):
        for t in range(4):
            base = 8 * pair + 2 * t
            above, below = vert[0, base].astype(F32), vert[1, base].astype(F32)
            rs[1, pair, t, 16:24, :] = jnp.where(low, below, above) * SCALE
            other = jnp.where(low, above, below)
            ub[0, pair, t] = pltpu.roll(other, 4, 0)
            ub[2, pair, t] = jnp.where(low, pltpu.roll(other, 1, 0), pltpu.roll(other, 7, 0))
            above, below = vert[0, base + 1].astype(F32), vert[1, base + 1].astype(F32)
            rs[0, pair, t, 16:24, :] = jnp.where(low, below, above) * SCALE
            ub[1, pair, t] = pltpu.roll(jnp.where(low, above, below), 4, 0)

    def strip(q, own, from_left, from_right):
        shape = own.shape
        small = iota(shape, 1) % 32
        even = ((iota(shape, 0) + small) % 2) == 0
        real0 = even if q % 2 == 0 else jnp.logical_not(even)
        real1 = jnp.logical_not(real0)
        back = (11, 2, 121, 11, 2)[q]
        take_left = ((small > 15) | ((small == 15) & real1)) & ((small < 19) | ((small == 19) & real0))
        take_right = ((small > 11) | ((small == 11) & real1)) & ((small < 15) | ((small == 15) & real0))
        return jnp.where(
            take_left,
            pltpu.roll(from_left, back, 1),
            jnp.where(take_right, pltpu.roll(from_right, back, 1), own),
        )

    def put(q, at, value):
        rows = value.shape[0]
        if q < 2:
            cs[q, 8 + at : 8 + at + rows, :] = value * SCALE
        else:
            ucs[q - 2, at : at + rows, :] = value

    def part_of(q):
        return 0 if q < 3 else 1

    for q in range(5):
        n = part_of(q)
        put(
            q,
            8,
            strip(q, merged[q].astype(F32), side[0, n].astype(F32), side[1, n].astype(F32)),
        )
        for end in range(2):
            put(
                q,
                0 if end == 0 else 136,
                strip(
                    q,
                    vert[end, 32 + q].astype(F32),
                    corner[2 * end, n].astype(F32),
                    corner[2 * end + 1, n].astype(F32),
                ),
            )
    put(5, 8, merged[5].astype(F32))

    def share(which):
        out = []
        for d in range(1, nrow):
            copy = pltpu.make_async_remote_copy(
                src_ref=red_send.at[which],
                dst_ref=red.at[d - 1, which],
                send_sem=red_send_sem.at[which, d - 1],
                recv_sem=red_recv_sem.at[which, d - 1],
                device_id=(gx, gy, peers[d - 1]),
                device_id_type=MESH,
            )
            copy.start()
            out.append(copy)
        return out

    def edge_part(which):
        p, q = 2 * which, 2 * which + 1
        even = jnp.concatenate([rsums[p, 1], rsums[p, 0]], axis=0)
        odd = jnp.concatenate([rsums[q, 1], rsums[q, 0]], axis=0)
        by_row = split_dot(jnp.where(wide_even, even, odd), pick[0]) + split_dot(
            jnp.where(wide_even, odd, even), pick[1]
        )
        even, odd = cs[0, 16:144, :], cs[1, 16:144, :]
        by_column = split_dot(jnp.where(tile_even, even, odd), edge_pick[0]) + split_dot(
            jnp.where(tile_even, odd, even), edge_pick[1]
        )
        top = by_column[0:8] + jnp.where(low, by_row[0:8], 0.0)
        bottom = by_column[120:128] + jnp.where(low, 0.0, by_row[8:16])
        by_column = jnp.concatenate([top, by_column[8:120], bottom], axis=0)
        return split_dot_left(rows_all, by_column)

    shared = []
    for s in range(4):
        x, y = s % 2, 1 - s % 2
        for part in range(3):
            if s == 3 and part == 1:
                continue
            u_of = (
                lambda pair, t: uu[s, pair, t, 120:128, :],
                lambda pair, t: ub[s, pair, t],
                lambda pair, t: uu[s, pair, t, 0:8, :],
            )[part]
            totals = update_rows(rs, s, 8 + 8 * part, range(4), u_of)
            if part != 1:
                for t in range(4):
                    rsums[s, part // 2, :, 128 * t : 128 * t + 128] = totals[t]
        for at in range(0, 144, 8):
            centre = cs[y, 8 + at : 16 + at, :]
            total = (
                cs[y, 7 + at : 15 + at, :]
                + cs[y, 9 + at : 17 + at, :]
                + pltpu.roll(centre, 1, 1)
                + pltpu.roll(centre, 127, 1)
            )
            cs[x, 8 + at : 16 + at, :] = new_value(
                cs[x, 8 + at : 16 + at, :], total, ucs[s, at : at + 8, :]
            )
        if s % 2 == 1:
            red_send[s // 2] = main_part[s // 2] + edge_part(s // 2)
            shared += share(s // 2)

    for copy in shared:
        copy.wait()
    for which in range(2):
        total = red_send[which]
        for d in range(1, nrow):
            total = total + red[d - 1, which]
        average_ref[which] = total * (1.0 / (SCALE * 8 * nrow * BLOCK * BLOCK))


def solution(mesh):
    sizes = tuple(mesh.shape[a] for a in ("gx", "gy", "row"))
    nrow = sizes[2]

    def per_device(occupancy, random_draws):
        any_space = pl.BlockSpec(memory_space=pl.ANY)
        vmem = pl.BlockSpec(memory_space=pltpu.VMEM)
        averages = pl.pallas_call(
            functools.partial(kernel, sizes),
            name="burst",
            out_shape=pltpu.VMEM((2, 32, 128), F32),
            in_specs=[any_space, any_space],
            out_specs=vmem,
            scratch_shapes=[
                pltpu.VMEM((8, 128, 512), jnp.int32),
                pltpu.VMEM((4, 8, 128, 512), BF16),
                pltpu.VMEM((2, 4, 4, 144, 128), F32),
                pltpu.VMEM((4, 4, 4, 128, 128), F32),
                pltpu.VMEM((4, 128, 512), F32),
                pltpu.VMEM((2, 4, 4, 40, 128), F32),
                pltpu.VMEM((3, 4, 4, 8, 128), F32),
                pltpu.VMEM((4, 2, 8, 512), F32),
                pltpu.VMEM((2, 160, 128), F32),
                pltpu.VMEM((4, 144, 128), F32),
                pltpu.VMEM((2, 1024, 128), BF16),
                pltpu.VMEM((2, 512, 128), BF16),
                pltpu.VMEM((2, 128, 128), BF16),
                pltpu.VMEM((6, 128, 128), BF16),
                pltpu.VMEM((2, 128, 128), BF16),
                pltpu.VMEM((2, 2, 128, 128), BF16),
                pltpu.VMEM((2, 2, 8, 128), BF16),
                pltpu.VMEM((4, 2, 8, 128), BF16),
                pltpu.VMEM((2, 37, 8, 128), BF16),
                pltpu.VMEM((2, 37, 8, 128), BF16),
                pltpu.VMEM((2, 32, 128), F32),
                pltpu.VMEM((2, 32, 128), F32),
                pltpu.VMEM((nrow - 1, 2, 32, 128), F32),
                pltpu.SemaphoreType.DMA((19,)),
                pltpu.SemaphoreType.DMA((8,)),
                pltpu.SemaphoreType.DMA((8,)),
                pltpu.SemaphoreType.DMA((2, nrow - 1)),
                pltpu.SemaphoreType.DMA((2, nrow - 1)),
            ],
            compiler_params=pltpu.CompilerParams(
                collective_id=0, has_side_effects=True, vmem_limit_bytes=62 * 1024 * 1024
            ),
        )(occupancy, random_draws)
        coverage = averages[1]
        return coverage, coverage + (LEAP / 2.0) * (coverage - averages[0])

    return jax.shard_map(
        per_device,
        mesh=mesh,
        in_specs=(P("row", "gx", "gy"), P(None, "row", "gx", "gy")),
        out_specs=(P("gx", "gy"), P("gx", "gy")),
        check_vma=False,
    )
```

```python
import functools

import jax
import jax.numpy as jnp
import numpy as np
from jax import lax
from jax.experimental import pallas as pl
from jax.experimental.pallas import tpu as pltpu
from jax.sharding import PartitionSpec as P

MESH = pl.DeviceIdType.MESH
BLOCK = 4
LEAP = 8
SCALE = float(-0.5 * np.log2(np.e))
F32 = jnp.float32
BF16 = jnp.bfloat16


def iota(shape, dim):
    return lax.broadcasted_iota(jnp.int32, shape, dim)


def new_value(x, total, u):
    gone = 0.6 - 0.6 * jnp.exp2(total)
    kept = x * gone
    return (0.1 * x + kept) + u * (0.6 * SCALE - kept) + 0.075 * total


def kernel(
    sizes,
    occ_hbm,
    u_hbm,
    average_ref,
    occ,
    draws,
    st,
    uu,
    sums,
    rs,
    ub,
    rsums,
    cs,
    ucs,
    place,
    pick,
    edge_pick,
    merged,
    side_send,
    side,
    corner_send,
    corner,
    vert_send,
    vert,
    main_part,
    red_send,
    red,
    load_sem,
    send_sem,
    recv_sem,
    red_send_sem,
    red_recv_sem,
):
    ngx, ngy, nrow = sizes
    gx, gy, row = lax.axis_index("gx"), lax.axis_index("gy"), lax.axis_index("row")
    up, down = lax.rem(gx + ngx - 1, ngx), lax.rem(gx + 1, ngx)
    left, right = lax.rem(gy + ngy - 1, ngy), lax.rem(gy + 1, ngy)

    loads = []

    def load(group, src, dst):
        copy = pltpu.make_async_copy(src, dst, load_sem.at[len(loads)])
        copy.start()
        loads.append((group, copy))

    def arrived(group):
        for which, copy in loads:
            if which == group:
                copy.wait()

    def load_occ(group, reals, rows, columns):
        at = (pl.ds(*reals), pl.ds(*rows), pl.ds(*columns))
        load(group, occ_hbm.at[at], occ.at[at])

    def load_u(group, sweeps, reals, rows, columns):
        at = (pl.ds(*sweeps), pl.ds(*reals), pl.ds(*rows), pl.ds(*columns))
        load(group, u_hbm.at[at], draws.at[at])

    for rows in ((0, 16), (112, 16)):
        load_occ("rows", (0, 8), rows, (0, 512))
        load_u("rows", (0, 3), (0, 8), rows, (0, 512))

    def load_columns():
        for columns in ((0, 128), (384, 128)):
            load_occ("columns", (0, 8), (16, 96), columns)
            load_u("columns", (0, 3), (0, 8), (16, 96), columns)

    def load_rest(pairs):
        for pair in pairs:
            load_occ("pair%d" % pair, (2 * pair, 2), (16, 96), (128, 256))
            load_u("pair%d" % pair, (0, 3), (2 * pair, 2), (16, 96), (128, 256))
            load_u("pair%d" % pair, (3, 1), (2 * pair, 2), (0, 128), (0, 512))

    load_columns()
    load_rest((0,))
    barrier = pltpu.get_barrier_semaphore()
    lattice = [
        (gx, left),
        (gx, right),
        (up, gy),
        (down, gy),
        (up, left),
        (up, right),
        (down, left),
        (down, right),
    ]
    for a, b in lattice:
        pl.semaphore_signal(barrier, inc=1, device_id=(a, b, row), device_id_type=MESH)
    peers = [lax.rem(row + d, nrow) for d in range(1, nrow)]
    for peer in peers:
        pl.semaphore_signal(barrier, inc=1, device_id=(gx, gy, peer), device_id_type=MESH)

    zeros8 = jnp.zeros((8, 128), F32)
    for which in range(2):
        for pair in range(4):
            for t in range(4):
                st[which, pair, t, 0:8, :] = zeros8
                st[which, pair, t, 136:144, :] = zeros8
                rs[which, pair, t, 0:8, :] = zeros8
                rs[which, pair, t, 32:40, :] = zeros8
        cs[which, 0:8, :] = zeros8
        cs[which, 152:160, :] = zeros8
    ucs[3, 0:8, :] = zeros8
    ucs[3, 136:144, :] = zeros8

    k = iota((256, 128), 0)
    far = k - 128
    for real in range(2):
        for pair in range(4):
            to = iota((256, 128), 1) - 32 * pair + real
            hit = ((k < 4) & (to == k + 12)) | ((k < 8) & (to == k + 20))
            hit |= ((far >= 120) & (to == far - 116)) | ((far >= 124) & (to == far - 108))
            place[real, 256 * pair : 256 * pair + 256, :] = jnp.where(hit, 1.0, 0.0).astype(BF16)
        column = iota((512, 128), 0) + real
        coarse = iota((512, 128), 1)
        hit = (coarse > 0) & (coarse < 127) & (column // BLOCK == coarse)
        pick[real] = jnp.where(hit, 1.0, 0.0).astype(BF16)
        small = iota((128, 128), 0) % 32 + real
        cell = iota((128, 128), 1)
        hit = ((cell == 127) & (small >= 8) & (small < 12)) | (
            (cell == 0) & (small >= 20) & (small < 24)
        )
        edge_pick[real] = jnp.where(hit, 1.0, 0.0).astype(BF16)

    sub = iota((8, 128), 0)
    low = sub < 4
    lane = iota((8, 128), 1)
    first_lane, last_lane = lane == 0, lane == 127
    wide_even = ((iota((16, 512), 0) + iota((16, 512), 1)) % 2) == 0
    tile_even = ((iota((128, 128), 0) + iota((128, 128), 1)) % 2) == 0

    def update_rows(array, s, at, pairs, u_of):
        x, y = s % 2, 1 - s % 2
        totals = [None] * 4
        for pair in pairs:
            centre = [array[y, pair, t, pl.ds(at, 8), :] for t in range(4)]
            on = [pltpu.roll(v, 1, 1) for v in centre]
            back = [pltpu.roll(v, 127, 1) for v in centre]
            for t in range(4):
                total = (
                    array[y, pair, t, pl.ds(at - 1, 8), :]
                    + array[y, pair, t, pl.ds(at + 1, 8), :]
                    + jnp.where(first_lane, on[(t + 3) % 4], on[t])
                    + jnp.where(last_lane, back[(t + 1) % 4], back[t])
                )
                value = new_value(array[x, pair, t, pl.ds(at, 8), :], total, u_of(pair, t))
                array[x, pair, t, pl.ds(at, 8), :] = value
                totals[t] = value if totals[t] is None else totals[t] + value
        return totals

    def chosen(first, shifted, even, which):
        return jnp.where(even, first, shifted) if which == 0 else jnp.where(even, shifted, first)

    def paired(first, second, even, which):
        return chosen(first, pltpu.roll(second, 511, 1), even, which)

    def pack(pair):
        def rows(c, carry):
            at = pl.multiple_of(c * 16, 16)
            first = occ[2 * pair, pl.ds(at, 16), :].astype(F32).astype(BF16)
            second = occ[2 * pair + 1, pl.ds(at, 16), :].astype(F32).astype(BF16)
            shifted = pltpu.roll(second, 511, 1)
            for which in range(2):
                both = chosen(first, shifted, wide_even, which).astype(F32) * SCALE
                for t in range(4):
                    st[which, pair, t, pl.ds(8 + at, 16), :] = both[:, 128 * t : 128 * t + 128]
            for s in range(4):
                first = draws[s, 2 * pair, pl.ds(at, 16), :]
                second = draws[s, 2 * pair + 1, pl.ds(at, 16), :]
                both = paired(first, second, wide_even, s % 2).astype(F32)
                for t in range(4):
                    uu[s, pair, t, pl.ds(at, 16), :] = both[:, 128 * t : 128 * t + 128]
            return carry

        lax.fori_loop(0, 8, rows, 0, unroll=4)
        for which in range(2):
            for t in range(4):
                rs[which, pair, t, 8:16, :] = st[which, pair, t, 128:136, :]
                rs[which, pair, t, 24:32, :] = st[which, pair, t, 8:16, :]

    def interior(pair):
        for s in range(4):

            def rows(c, carry, s=s):
                at = pl.multiple_of(c * 8, 8)
                totals = update_rows(
                    st, s, 8 + at, (pair,), lambda p, t: uu[s, p, t, pl.ds(at, 8), :]
                )
                for t in range(4):
                    if pair == 0:
                        sums[s, t, pl.ds(at, 8), :] = totals[t]
                    else:
                        sums[s, t, pl.ds(at, 8), :] += totals[t]
                return carry

            lax.fori_loop(0, 16, rows, 0, unroll=16)

    arrived("rows")
    load_rest((1, 2, 3))

    def edge_columns(real, load_real):
        tiles = []
        for pair in range(4):
            tiles += [load_real(2 * pair + real, 0), load_real(2 * pair + real, 384)]
        return jnp.dot(
            jnp.concatenate(tiles, axis=1), place[real], preferred_element_type=F32
        )

    def occupied(rows):
        return [
            edge_columns(r, lambda i, c: occ[i, rows, c : c + 128].astype(F32).astype(BF16))
            for r in (0, 1)
        ]

    def drawn(s, rows):
        return [edge_columns(r, lambda i, c: draws[s, i, rows, c : c + 128]) for r in (0, 1)]

    def strips_of(rows):
        even = tile_even[0 : rows.stop - rows.start]
        real0, real1 = occupied(rows)
        strips = [jnp.where(even, real0, real1), jnp.where(even, real1, real0)]
        for s in range(3):
            pair = drawn(s, rows)
            strips.append(jnp.where(even, pair[s % 2], pair[1 - s % 2]))
        return strips

    def squeezed(strips):
        slot = (iota(strips[0].shape, 1) % 32) // 9
        return (
            jnp.where(
                slot == 0,
                pltpu.roll(strips[0], 117, 1),
                jnp.where(slot == 1, pltpu.roll(strips[1], 126, 1), pltpu.roll(strips[2], 7, 1)),
            ),
            jnp.where(slot == 0, pltpu.roll(strips[3], 117, 1), pltpu.roll(strips[4], 126, 1)),
        )

    def send(slot, src, dst, a, b):
        copy = pltpu.make_async_remote_copy(
            src_ref=src,
            dst_ref=dst,
            send_sem=send_sem.at[slot],
            recv_sem=recv_sem.at[slot],
            device_id=(a, b, row),
            device_id_type=MESH,
        )
        copy.start()
        return copy

    for end in range(2):
        strips = strips_of(slice(0, 16) if end == 0 else slice(112, 128))
        keep = slice(0, 8) if end == 0 else slice(8, 16)
        for part, value in enumerate(squeezed(strips)):
            corner_send[end, part] = value[keep].astype(BF16)
        for q in range(5):
            vert_send[end, 32 + q] = strips[q][keep].astype(BF16)

    even8 = wide_even[0:8]
    sub_wide = iota((8, 512), 0)
    for end in range(2):
        at = 0 if end == 0 else 112
        keep = slice(0, 8) if end == 0 else slice(8, 16)
        mine = sub_wide < 4 if end == 0 else sub_wide >= 4
        outer = sub_wide == (7 if end == 0 else 0)
        for pair in range(4):
            first = occ[2 * pair, at : at + 16, :][keep].astype(F32)
            second = occ[2 * pair + 1, at : at + 16, :][keep].astype(F32)
            p, q = paired(first, second, even8, 0), paired(first, second, even8, 1)
            u = [
                paired(
                    draws[s, 2 * pair, at : at + 16, :].astype(F32)[keep],
                    draws[s, 2 * pair + 1, at : at + 16, :].astype(F32)[keep],
                    even8,
                    s % 2,
                )
                for s in range(3)
            ]
            tiles = (
                jnp.where(
                    mine,
                    q,
                    jnp.where(outer, pltpu.roll(u[2], 7 if end == 0 else 1, 0), pltpu.roll(u[0], 4, 0)),
                ),
                jnp.where(mine, p, pltpu.roll(u[1], 4, 0)),
            )
            for n in range(2):
                packed = tiles[n].astype(BF16)
                for t in range(4):
                    vert_send[end, 8 * pair + 2 * t + n] = packed[:, 128 * t : 128 * t + 128]

    arrived("columns")
    strips = strips_of(slice(0, 128))
    for q in range(5):
        merged[q] = strips[q].astype(BF16)
    for part, value in enumerate(squeezed(strips)):
        side_send[part] = value.astype(BF16)
    pl.semaphore_wait(barrier, 8 + nrow - 1)
    corner_copies = [
        send(4, corner_send.at[1], corner.at[0], down, right),
        send(5, corner_send.at[1], corner.at[1], down, left),
        send(6, corner_send.at[0], corner.at[2], up, right),
        send(7, corner_send.at[0], corner.at[3], up, left),
    ]

    row_copies = [
        send(2, vert_send.at[1], vert.at[0], down, gy),
        send(3, vert_send.at[0], vert.at[1], up, gy),
    ]
    column_copies = [
        send(0, side_send, side.at[0], gx, right),
        send(1, side_send, side.at[1], gx, left),
    ]

    for pair in range(4):
        arrived("pair%d" % pair)
        pack(pair)
        interior(pair)
    real0, real1 = drawn(3, slice(0, 128))
    last_strip = jnp.where(tile_even, real1, real0)
    ucs[3, 8:136, :] = last_strip

    lane32 = iota((32, 128), 1)
    row32 = iota((32, 128), 0)
    inner = (row32 > 0) & (row32 < 31)

    def cell_rows(p_of, q_of):
        real0, real1 = 0.0, 0.0
        for k in range(4):
            even, p, q = (lane32 + k) % 2 == 0, p_of(k), q_of(k)
            real0 += jnp.where(even, p, q)
            real1 += jnp.where(even, q, p)
        return real0, real1

    def halves(x):
        high = x.astype(BF16).astype(F32)
        return [high, x - high]

    def dots(pieces, tables):
        return sum(
            jnp.dot(
                jnp.concatenate(pieces[real], axis=0).astype(BF16),
                tables[real],
                preferred_element_type=F32,
            )
            for real in range(2)
        )

    pieces = ([], [])
    for which in range(2):
        tiles = ([], [])
        for t in range(4):
            both = cell_rows(
                lambda k: sums[2 * which, t, pl.ds(k, 32, stride=4), :],
                lambda k: sums[2 * which + 1, t, pl.ds(k, 32, stride=4), :],
            )
            for real in range(2):
                tiles[real].append(jnp.where(inner, both[real], 0.0))
        for real in range(2):
            pieces[real].extend(halves(jnp.concatenate(tiles[real], axis=1)))
    by_cell = dots(pieces, pick)
    for which in range(2):
        at = 64 * which
        main_part[which] = by_cell[at : at + 32] + by_cell[at + 32 : at + 64]

    for copy in row_copies:
        copy.wait()

    for pair in range(4):
        for t in range(4):
            base = 8 * pair + 2 * t
            above, below = vert[0, base].astype(F32), vert[1, base].astype(F32)
            rs[1, pair, t, 16:24, :] = jnp.where(low, below, above) * SCALE
            other = jnp.where(low, above, below)
            ub[0, pair, t] = pltpu.roll(other, 4, 0)
            ub[2, pair, t] = jnp.where(low, pltpu.roll(other, 1, 0), pltpu.roll(other, 7, 0))
            above, below = vert[0, base + 1].astype(F32), vert[1, base + 1].astype(F32)
            rs[0, pair, t, 16:24, :] = jnp.where(low, below, above) * SCALE
            ub[1, pair, t] = pltpu.roll(jnp.where(low, above, below), 4, 0)

    for copy in corner_copies + column_copies:
        copy.wait()

    def strip(q, own, from_left, from_right):
        shape = own.shape
        small = iota(shape, 1) % 32
        even = ((iota(shape, 0) + small) % 2) == 0
        real0 = even if q % 2 == 0 else jnp.logical_not(even)
        real1 = jnp.logical_not(real0)
        back = (11, 2, 121, 11, 2)[q]
        take_left = ((small > 15) | ((small == 15) & real1)) & ((small < 19) | ((small == 19) & real0))
        take_right = ((small > 11) | ((small == 11) & real1)) & ((small < 15) | ((small == 15) & real0))
        return jnp.where(
            take_left,
            pltpu.roll(from_left, back, 1),
            jnp.where(take_right, pltpu.roll(from_right, back, 1), own),
        )

    def put(q, at, value):
        rows = value.shape[0]
        if q < 2:
            cs[q, 8 + at : 8 + at + rows, :] = value * SCALE
        else:
            ucs[q - 2, at : at + rows, :] = value

    def part_of(q):
        return 0 if q < 3 else 1

    for q in range(5):
        n = part_of(q)
        put(
            q,
            8,
            strip(q, merged[q].astype(F32), side[0, n].astype(F32), side[1, n].astype(F32)),
        )
        for end in range(2):
            put(
                q,
                0 if end == 0 else 136,
                strip(
                    q,
                    vert[end, 32 + q].astype(F32),
                    corner[2 * end, n].astype(F32),
                    corner[2 * end + 1, n].astype(F32),
                ),
            )

    def share(which):
        out = []
        for d in range(1, nrow):
            copy = pltpu.make_async_remote_copy(
                src_ref=red_send.at[which],
                dst_ref=red.at[d - 1, which],
                send_sem=red_send_sem.at[which, d - 1],
                recv_sem=red_recv_sem.at[which, d - 1],
                device_id=(gx, gy, peers[d - 1]),
                device_id_type=MESH,
            )
            copy.start()
            out.append(copy)
        return out

    def edge_part(which):
        p, q = 2 * which, 2 * which + 1
        both = cell_rows(
            lambda k: cs[0, pl.ds(16 + k, 32, stride=4), :],
            lambda k: cs[1, pl.ds(16 + k, 32, stride=4), :],
        )
        by_cell = dots([halves(both[0]), halves(both[1])], edge_pick)
        by_cell = by_cell[0:32] + by_cell[32:64]
        low_wide = sub_wide < 4
        p = jnp.where(low_wide, rsums[p, 1], rsums[p, 0])
        q = jnp.where(low_wide, rsums[q, 1], rsums[q, 0])
        pieces = []
        for real in range(2):
            x = chosen(p, q, even8, real)
            x = x + pltpu.roll(x, 7, 0)
            x = x + pltpu.roll(x, 6, 0)
            pieces.append(halves(x))
        by_row = dots(pieces, pick)
        by_row = by_row[0:8] + by_row[8:16]
        top = by_cell[0:8] + jnp.where(sub == 0, by_row, 0.0)
        bottom = by_cell[24:32] + jnp.where(sub == 7, pltpu.roll(by_row, 3, 0), 0.0)
        return jnp.concatenate([top, by_cell[8:24], bottom], axis=0)

    shared = []
    for s in range(4):
        x, y = s % 2, 1 - s % 2
        for part in range(3):
            if s == 3 and part == 1:
                continue
            u_of = (
                lambda pair, t: uu[s, pair, t, 120:128, :],
                lambda pair, t: ub[s, pair, t],
                lambda pair, t: uu[s, pair, t, 0:8, :],
            )[part]
            totals = update_rows(rs, s, 8 + 8 * part, range(4), u_of)
            if part != 1:
                for t in range(4):
                    rsums[s, part // 2, :, 128 * t : 128 * t + 128] = totals[t]
        for at in range(0, 144, 8):
            centre = cs[y, 8 + at : 16 + at, :]
            total = (
                cs[y, 7 + at : 15 + at, :]
                + cs[y, 9 + at : 17 + at, :]
                + pltpu.roll(centre, 1, 1)
                + pltpu.roll(centre, 127, 1)
            )
            cs[x, 8 + at : 16 + at, :] = new_value(
                cs[x, 8 + at : 16 + at, :], total, ucs[s, at : at + 8, :]
            )
        if s % 2 == 1:
            red_send[s // 2] = main_part[s // 2] + edge_part(s // 2)
            shared += share(s // 2)

    for copy in shared:
        copy.wait()
    for which in range(2):
        total = red_send[which]
        for d in range(1, nrow):
            total = total + red[d - 1, which]
        average_ref[which] = total * (1.0 / (SCALE * 8 * nrow * BLOCK * BLOCK))


def solution(mesh):
    sizes = tuple(mesh.shape[a] for a in ("gx", "gy", "row"))
    nrow = sizes[2]

    def per_device(occupancy, random_draws):
        any_space = pl.BlockSpec(memory_space=pl.ANY)
        vmem = pl.BlockSpec(memory_space=pltpu.VMEM)
        averages = pl.pallas_call(
            functools.partial(kernel, sizes),
            name="burst",
            out_shape=pltpu.VMEM((2, 32, 128), F32),
            in_specs=[any_space, any_space],
            out_specs=vmem,
            scratch_shapes=[
                pltpu.VMEM((8, 128, 512), jnp.int32),
                pltpu.VMEM((4, 8, 128, 512), BF16),
                pltpu.VMEM((2, 4, 4, 144, 128), F32),
                pltpu.VMEM((4, 4, 4, 128, 128), F32),
                pltpu.VMEM((4, 4, 128, 128), F32),
                pltpu.VMEM((2, 4, 4, 40, 128), F32),
                pltpu.VMEM((3, 4, 4, 8, 128), F32),
                pltpu.VMEM((4, 2, 8, 512), F32),
                pltpu.VMEM((2, 160, 128), F32),
                pltpu.VMEM((4, 144, 128), F32),
                pltpu.VMEM((2, 1024, 128), BF16),
                pltpu.VMEM((2, 512, 128), BF16),
                pltpu.VMEM((2, 128, 128), BF16),
                pltpu.VMEM((5, 128, 128), BF16),
                pltpu.VMEM((2, 128, 128), BF16),
                pltpu.VMEM((2, 2, 128, 128), BF16),
                pltpu.VMEM((2, 2, 8, 128), BF16),
                pltpu.VMEM((4, 2, 8, 128), BF16),
                pltpu.VMEM((2, 37, 8, 128), BF16),
                pltpu.VMEM((2, 37, 8, 128), BF16),
                pltpu.VMEM((2, 32, 128), F32),
                pltpu.VMEM((2, 32, 128), F32),
                pltpu.VMEM((nrow - 1, 2, 32, 128), F32),
                pltpu.SemaphoreType.DMA((20,)),
                pltpu.SemaphoreType.DMA((8,)),
                pltpu.SemaphoreType.DMA((8,)),
                pltpu.SemaphoreType.DMA((2, nrow - 1)),
                pltpu.SemaphoreType.DMA((2, nrow - 1)),
            ],
            compiler_params=pltpu.CompilerParams(
                collective_id=0, has_side_effects=True, vmem_limit_bytes=62 * 1024 * 1024
            ),
        )(occupancy, random_draws)
        coverage = averages[1]
        return coverage, coverage + (LEAP / 2.0) * (coverage - averages[0])

    return jax.shard_map(
        per_device,
        mesh=mesh,
        in_specs=(P("row", "gx", "gy"), P(None, "row", "gx", "gy")),
        out_specs=(P("gx", "gy"), P("gx", "gy")),
        check_vma=False,
    )
```

```python
import functools

import jax
import jax.numpy as jnp
import numpy as np
from jax import lax
from jax.experimental import pallas as pl
from jax.experimental.pallas import tpu as pltpu
from jax.sharding import PartitionSpec as P

MESH = pl.DeviceIdType.MESH
BLOCK = 4
LEAP = 8
SCALE = float(-0.5 * np.log2(np.e))
F32 = jnp.float32
BF16 = jnp.bfloat16


def iota(shape, dim):
    return lax.broadcasted_iota(jnp.int32, shape, dim)


def new_value(x, total, u):
    gone = 0.6 - 0.6 * jnp.exp2(total)
    kept = x * gone
    return (0.1 * x + kept) + u * (0.6 * SCALE - kept) + 0.075 * total


def kernel(
    sizes,
    occ_hbm,
    u_hbm,
    average_ref,
    occ,
    draws,
    st,
    uu,
    sums,
    rs,
    ub,
    rsums,
    cs,
    ucs,
    place,
    pick,
    edge_pick,
    merged,
    side_send,
    side,
    corner_send,
    corner,
    vert_send,
    vert,
    main_part,
    red_main,
    edge_send,
    red_edge,
    load_sem,
    send_sem,
    recv_sem,
    red_send_sem,
    red_recv_sem,
):
    ngx, ngy, nrow = sizes
    gx, gy, row = lax.axis_index("gx"), lax.axis_index("gy"), lax.axis_index("row")
    up, down = lax.rem(gx + ngx - 1, ngx), lax.rem(gx + 1, ngx)
    left, right = lax.rem(gy + ngy - 1, ngy), lax.rem(gy + 1, ngy)

    loads = []

    def load(group, src, dst):
        copy = pltpu.make_async_copy(src, dst, load_sem.at[len(loads)])
        copy.start()
        loads.append((group, copy))

    def arrived(group):
        for which, copy in loads:
            if which == group:
                copy.wait()

    def load_occ(group, reals, rows, columns):
        at = (pl.ds(*reals), pl.ds(*rows), pl.ds(*columns))
        load(group, occ_hbm.at[at], occ.at[at])

    def load_u(group, sweeps, reals, rows, columns):
        at = (pl.ds(*sweeps), pl.ds(*reals), pl.ds(*rows), pl.ds(*columns))
        load(group, u_hbm.at[at], draws.at[at])

    for rows in ((0, 16), (112, 16)):
        load_occ("rows", (0, 8), rows, (0, 512))
        load_u("rows", (0, 3), (0, 8), rows, (0, 512))

    def load_columns():
        for columns in ((0, 128), (384, 128)):
            load_occ("columns", (0, 8), (16, 96), columns)
            load_u("columns", (0, 3), (0, 8), (16, 96), columns)

    def load_rest(pairs):
        for pair in pairs:
            load_occ("pair%d" % pair, (2 * pair, 2), (16, 96), (128, 256))
            load_u("pair%d" % pair, (0, 3), (2 * pair, 2), (16, 96), (128, 256))
            load_u("pair%d" % pair, (3, 1), (2 * pair, 2), (0, 128), (0, 512))

    load_columns()
    load_rest((0,))
    barrier = pltpu.get_barrier_semaphore()
    lattice = [
        (gx, left),
        (gx, right),
        (up, gy),
        (down, gy),
        (up, left),
        (up, right),
        (down, left),
        (down, right),
    ]
    for a, b in lattice:
        pl.semaphore_signal(barrier, inc=1, device_id=(a, b, row), device_id_type=MESH)
    peers = [lax.rem(row + d, nrow) for d in range(1, nrow)]
    for peer in peers:
        pl.semaphore_signal(barrier, inc=1, device_id=(gx, gy, peer), device_id_type=MESH)

    zeros8 = jnp.zeros((8, 128), F32)
    for which in range(2):
        for pair in range(4):
            for t in range(4):
                st[which, pair, t, 0:8, :] = zeros8
                st[which, pair, t, 136:144, :] = zeros8
                rs[which, pair, t, 0:8, :] = zeros8
                rs[which, pair, t, 32:40, :] = zeros8
        cs[which, 0:8, :] = zeros8
        cs[which, 152:160, :] = zeros8
    ucs[3, 0:8, :] = zeros8
    ucs[3, 136:144, :] = zeros8

    k = iota((256, 128), 0)
    far = k - 128
    for real in range(2):
        for pair in range(4):
            to = iota((256, 128), 1) - 32 * pair + real
            hit = ((k < 4) & (to == k + 12)) | ((k < 8) & (to == k + 20))
            hit |= ((far >= 120) & (to == far - 116)) | ((far >= 124) & (to == far - 108))
            place[real, 256 * pair : 256 * pair + 256, :] = jnp.where(hit, 1.0, 0.0).astype(BF16)
        column = iota((512, 128), 0) + real
        coarse = iota((512, 128), 1)
        hit = (coarse > 0) & (coarse < 127) & (column // BLOCK == coarse)
        pick[real] = jnp.where(hit, 1.0, 0.0).astype(BF16)
        small = iota((128, 128), 0) % 32 + real
        cell = iota((128, 128), 1)
        hit = ((cell == 127) & (small >= 8) & (small < 12)) | (
            (cell == 0) & (small >= 20) & (small < 24)
        )
        edge_pick[real] = jnp.where(hit, 1.0, 0.0).astype(BF16)

    sub = iota((8, 128), 0)
    low = sub < 4
    lane = iota((8, 128), 1)
    first_lane, last_lane = lane == 0, lane == 127
    wide_even = ((iota((16, 512), 0) + iota((16, 512), 1)) % 2) == 0
    tile_even = ((iota((128, 128), 0) + iota((128, 128), 1)) % 2) == 0

    def update_rows(array, s, at, pairs, u_of):
        x, y = s % 2, 1 - s % 2
        totals = [None] * 4
        for pair in pairs:
            centre = [array[y, pair, t, pl.ds(at, 8), :] for t in range(4)]
            on = [pltpu.roll(v, 1, 1) for v in centre]
            back = [pltpu.roll(v, 127, 1) for v in centre]
            for t in range(4):
                total = (
                    array[y, pair, t, pl.ds(at - 1, 8), :]
                    + array[y, pair, t, pl.ds(at + 1, 8), :]
                    + jnp.where(first_lane, on[(t + 3) % 4], on[t])
                    + jnp.where(last_lane, back[(t + 1) % 4], back[t])
                )
                value = new_value(array[x, pair, t, pl.ds(at, 8), :], total, u_of(pair, t))
                array[x, pair, t, pl.ds(at, 8), :] = value
                totals[t] = value if totals[t] is None else totals[t] + value
        return totals

    def chosen(first, shifted, even, which):
        return jnp.where(even, first, shifted) if which == 0 else jnp.where(even, shifted, first)

    def paired(first, second, even, which):
        return chosen(first, pltpu.roll(second, 511, 1), even, which)

    def pack(pair):
        def rows(c, carry):
            at = pl.multiple_of(c * 16, 16)
            first = occ[2 * pair, pl.ds(at, 16), :].astype(F32).astype(BF16)
            second = occ[2 * pair + 1, pl.ds(at, 16), :].astype(F32).astype(BF16)
            shifted = pltpu.roll(second, 511, 1)
            for which in range(2):
                both = chosen(first, shifted, wide_even, which).astype(F32) * SCALE
                for t in range(4):
                    st[which, pair, t, pl.ds(8 + at, 16), :] = both[:, 128 * t : 128 * t + 128]
            return carry

        lax.fori_loop(0, 8, rows, 0, unroll=8)
        for which in range(2):
            for t in range(4):
                rs[which, pair, t, 8:16, :] = st[which, pair, t, 128:136, :]
                rs[which, pair, t, 24:32, :] = st[which, pair, t, 8:16, :]

    def interior(pair):
        for s in range(4):
            for at in range(0, 128, 16):
                u = paired(
                    draws[s, 2 * pair, at : at + 16, :],
                    draws[s, 2 * pair + 1, at : at + 16, :],
                    wide_even,
                    s % 2,
                ).astype(F32)
                for half in (0, 8):
                    here = [u[half : half + 8, 128 * t : 128 * t + 128] for t in range(4)]
                    if at + half in (0, 120):
                        for t in range(4):
                            uu[(at + half) // 120, s, pair, t] = here[t]
                    totals = update_rows(st, s, 8 + at + half, (pair,), lambda p, t: here[t])
                    for t in range(4):
                        if pair == 0:
                            sums[s, t, pl.ds(at + half, 8), :] = totals[t]
                        else:
                            sums[s, t, pl.ds(at + half, 8), :] += totals[t]

    arrived("rows")
    load_rest((1, 2, 3))

    def edge_columns(real, load_real):
        tiles = []
        for pair in range(4):
            tiles += [load_real(2 * pair + real, 0), load_real(2 * pair + real, 384)]
        return jnp.dot(
            jnp.concatenate(tiles, axis=1), place[real], preferred_element_type=F32
        )

    def occupied(rows):
        return [
            edge_columns(r, lambda i, c: occ[i, rows, c : c + 128].astype(F32).astype(BF16))
            for r in (0, 1)
        ]

    def drawn(s, rows):
        return [edge_columns(r, lambda i, c: draws[s, i, rows, c : c + 128]) for r in (0, 1)]

    def strips_of(rows):
        even = tile_even[0 : rows.stop - rows.start]
        real0, real1 = occupied(rows)
        strips = [jnp.where(even, real0, real1), jnp.where(even, real1, real0)]
        for s in range(3):
            pair = drawn(s, rows)
            strips.append(jnp.where(even, pair[s % 2], pair[1 - s % 2]))
        return strips

    def squeezed(strips):
        slot = (iota(strips[0].shape, 1) % 32) // 9
        return (
            jnp.where(
                slot == 0,
                pltpu.roll(strips[0], 117, 1),
                jnp.where(slot == 1, pltpu.roll(strips[1], 126, 1), pltpu.roll(strips[2], 7, 1)),
            ),
            jnp.where(slot == 0, pltpu.roll(strips[3], 117, 1), pltpu.roll(strips[4], 126, 1)),
        )

    def send(slot, src, dst, a, b):
        copy = pltpu.make_async_remote_copy(
            src_ref=src,
            dst_ref=dst,
            send_sem=send_sem.at[slot],
            recv_sem=recv_sem.at[slot],
            device_id=(a, b, row),
            device_id_type=MESH,
        )
        copy.start()
        return copy

    for end in range(2):
        strips = strips_of(slice(0, 16) if end == 0 else slice(112, 128))
        keep = slice(0, 8) if end == 0 else slice(8, 16)
        for part, value in enumerate(squeezed(strips)):
            corner_send[end, part] = value[keep].astype(BF16)
        for q in range(5):
            vert_send[end, 32 + q] = strips[q][keep].astype(BF16)

    even8 = wide_even[0:8]
    sub_wide = iota((8, 512), 0)
    for end in range(2):
        at = 0 if end == 0 else 112
        keep = slice(0, 8) if end == 0 else slice(8, 16)
        mine = sub_wide < 4 if end == 0 else sub_wide >= 4
        outer = sub_wide == (7 if end == 0 else 0)
        for pair in range(4):
            first = occ[2 * pair, at : at + 16, :][keep].astype(F32)
            second = occ[2 * pair + 1, at : at + 16, :][keep].astype(F32)
            p, q = paired(first, second, even8, 0), paired(first, second, even8, 1)
            u = [
                paired(
                    draws[s, 2 * pair, at : at + 16, :].astype(F32)[keep],
                    draws[s, 2 * pair + 1, at : at + 16, :].astype(F32)[keep],
                    even8,
                    s % 2,
                )
                for s in range(3)
            ]
            tiles = (
                jnp.where(
                    mine,
                    q,
                    jnp.where(outer, pltpu.roll(u[2], 7 if end == 0 else 1, 0), pltpu.roll(u[0], 4, 0)),
                ),
                jnp.where(mine, p, pltpu.roll(u[1], 4, 0)),
            )
            for n in range(2):
                packed = tiles[n].astype(BF16)
                for t in range(4):
                    vert_send[end, 8 * pair + 2 * t + n] = packed[:, 128 * t : 128 * t + 128]

    arrived("columns")
    strips = strips_of(slice(0, 128))
    for q in range(5):
        merged[q] = strips[q].astype(BF16)
    for part, value in enumerate(squeezed(strips)):
        side_send[part] = value.astype(BF16)
    pl.semaphore_wait(barrier, 8 + nrow - 1)
    corner_copies = [
        send(4, corner_send.at[1], corner.at[0], down, right),
        send(5, corner_send.at[1], corner.at[1], down, left),
        send(6, corner_send.at[0], corner.at[2], up, right),
        send(7, corner_send.at[0], corner.at[3], up, left),
    ]

    row_copies = [
        send(2, vert_send.at[1], vert.at[0], down, gy),
        send(3, vert_send.at[0], vert.at[1], up, gy),
    ]
    column_copies = [
        send(0, side_send, side.at[0], gx, right),
        send(1, side_send, side.at[1], gx, left),
    ]

    for pair in range(4):
        arrived("pair%d" % pair)
        pack(pair)
        interior(pair)
    real0, real1 = drawn(3, slice(0, 128))
    last_strip = jnp.where(tile_even, real1, real0)
    ucs[3, 8:136, :] = last_strip

    lane32 = iota((32, 128), 1)
    row32 = iota((32, 128), 0)
    inner = (row32 > 0) & (row32 < 31)

    def cell_rows(p_of, q_of):
        real0, real1 = 0.0, 0.0
        for k in range(4):
            even, p, q = (lane32 + k) % 2 == 0, p_of(k), q_of(k)
            real0 += jnp.where(even, p, q)
            real1 += jnp.where(even, q, p)
        return real0, real1

    def halves(x):
        high = x.astype(BF16).astype(F32)
        return [high, x - high]

    def dots(pieces, tables):
        return sum(
            jnp.dot(
                jnp.concatenate(pieces[real], axis=0).astype(BF16),
                tables[real],
                preferred_element_type=F32,
            )
            for real in range(2)
        )

    pieces = ([], [])
    for which in range(2):
        tiles = ([], [])
        for t in range(4):
            both = cell_rows(
                lambda k: sums[2 * which, t, pl.ds(k, 32, stride=4), :],
                lambda k: sums[2 * which + 1, t, pl.ds(k, 32, stride=4), :],
            )
            for real in range(2):
                tiles[real].append(jnp.where(inner, both[real], 0.0))
        for real in range(2):
            pieces[real].extend(halves(jnp.concatenate(tiles[real], axis=1)))
    by_cell = dots(pieces, pick)
    for which in range(2):
        at = 64 * which
        main_part[which] = by_cell[at : at + 32] + by_cell[at + 32 : at + 64]

    def share(stage, src, dst):
        out = []
        for d in range(1, nrow):
            copy = pltpu.make_async_remote_copy(
                src_ref=src,
                dst_ref=dst.at[d - 1],
                send_sem=red_send_sem.at[stage, d - 1],
                recv_sem=red_recv_sem.at[stage, d - 1],
                device_id=(gx, gy, peers[d - 1]),
                device_id_type=MESH,
            )
            copy.start()
            out.append(copy)
        return out

    shared = share(0, main_part, red_main)

    for copy in row_copies:
        copy.wait()

    for pair in range(4):
        for t in range(4):
            base = 8 * pair + 2 * t
            above, below = vert[0, base].astype(F32), vert[1, base].astype(F32)
            rs[1, pair, t, 16:24, :] = jnp.where(low, below, above) * SCALE
            other = jnp.where(low, above, below)
            ub[0, pair, t] = pltpu.roll(other, 4, 0)
            ub[2, pair, t] = jnp.where(low, pltpu.roll(other, 1, 0), pltpu.roll(other, 7, 0))
            above, below = vert[0, base + 1].astype(F32), vert[1, base + 1].astype(F32)
            rs[0, pair, t, 16:24, :] = jnp.where(low, below, above) * SCALE
            ub[1, pair, t] = pltpu.roll(jnp.where(low, above, below), 4, 0)

    for copy in corner_copies + column_copies:
        copy.wait()

    def strip(q, own, from_left, from_right):
        shape = own.shape
        small = iota(shape, 1) % 32
        even = ((iota(shape, 0) + small) % 2) == 0
        real0 = even if q % 2 == 0 else jnp.logical_not(even)
        real1 = jnp.logical_not(real0)
        back = (11, 2, 121, 11, 2)[q]
        take_left = ((small > 15) | ((small == 15) & real1)) & ((small < 19) | ((small == 19) & real0))
        take_right = ((small > 11) | ((small == 11) & real1)) & ((small < 15) | ((small == 15) & real0))
        return jnp.where(
            take_left,
            pltpu.roll(from_left, back, 1),
            jnp.where(take_right, pltpu.roll(from_right, back, 1), own),
        )

    def put(q, at, value):
        rows = value.shape[0]
        if q < 2:
            cs[q, 8 + at : 8 + at + rows, :] = value * SCALE
        else:
            ucs[q - 2, at : at + rows, :] = value

    def part_of(q):
        return 0 if q < 3 else 1

    for q in range(5):
        n = part_of(q)
        put(
            q,
            8,
            strip(q, merged[q].astype(F32), side[0, n].astype(F32), side[1, n].astype(F32)),
        )
        for end in range(2):
            put(
                q,
                0 if end == 0 else 136,
                strip(
                    q,
                    vert[end, 32 + q].astype(F32),
                    corner[2 * end, n].astype(F32),
                    corner[2 * end + 1, n].astype(F32),
                ),
            )

    end_lane = (lane32 == 0) | (lane32 == 127)

    def turned(x, amount, dim):
        return pltpu.roll(x, amount % x.shape[dim], dim) if amount % x.shape[dim] else x

    def edge_part(which):
        p, q = 2 * which, 2 * which + 1
        both = cell_rows(
            lambda k: cs[0, pl.ds(16 + k, 32, stride=4), :],
            lambda k: cs[1, pl.ds(16 + k, 32, stride=4), :],
        )
        by_cell = dots([halves(both[0]), halves(both[1])], edge_pick)
        by_cell = by_cell[0:32] + by_cell[32:64]
        low_wide = sub_wide < 4
        p = jnp.where(low_wide, rsums[p, 1], rsums[p, 0])
        q = jnp.where(low_wide, rsums[q, 1], rsums[q, 0])
        pieces = []
        for real in range(2):
            x = chosen(p, q, even8, real)
            x = x + pltpu.roll(x, 7, 0)
            x = x + pltpu.roll(x, 6, 0)
            pieces.append(halves(x))
        by_row = dots(pieces, pick)
        by_row = by_row[0:8] + by_row[8:16]
        ends = jnp.where(end_lane, by_cell, 0.0)
        columns = sum(
            turned(ends[8 * k : 8 * k + 8], 2 * (4 * which + k), 1) for k in range(4)
        )
        return columns, turned(jnp.where((sub == 0) | (sub == 4), by_row, 0.0), which, 0)

    edges = []
    for s in range(4):
        x, y = s % 2, 1 - s % 2
        for part in range(3):
            if s == 3 and part == 1:
                continue
            u_of = (
                lambda pair, t: uu[1, s, pair, t],
                lambda pair, t: ub[s, pair, t],
                lambda pair, t: uu[0, s, pair, t],
            )[part]
            totals = update_rows(rs, s, 8 + 8 * part, range(4), u_of)
            if part != 1:
                for t in range(4):
                    rsums[s, part // 2, :, 128 * t : 128 * t + 128] = totals[t]
        for at in range(0, 144, 8):
            centre = cs[y, 8 + at : 16 + at, :]
            total = (
                cs[y, 7 + at : 15 + at, :]
                + cs[y, 9 + at : 17 + at, :]
                + pltpu.roll(centre, 1, 1)
                + pltpu.roll(centre, 127, 1)
            )
            cs[x, 8 + at : 16 + at, :] = new_value(
                cs[x, 8 + at : 16 + at, :], total, ucs[s, at : at + 8, :]
            )
        if s % 2 == 1:
            edges.append(edge_part(s // 2))
    for k in range(2):
        edge_send[k] = edges[0][k] + edges[1][k]
    shared += share(1, edge_send, red_edge)

    for copy in shared:
        copy.wait()
    columns, rows = edge_send[0], edge_send[1]
    for d in range(nrow - 1):
        columns, rows = columns + red_edge[d, 0], rows + red_edge[d, 1]
    scale = 1.0 / (SCALE * 8 * nrow * BLOCK * BLOCK)
    for which in range(2):
        total = main_part[which]
        for d in range(nrow - 1):
            total = total + red_main[d, which]
        for k in range(4):
            part = total[8 * k : 8 * k + 8] + jnp.where(
                end_lane[0:8], turned(columns, -2 * (4 * which + k), 1), 0.0
            )
            if k == 0:
                part = part + jnp.where(sub == 0, turned(rows, -which, 0), 0.0)
            if k == 3:
                part = part + jnp.where(sub == 7, turned(rows, 3 - which, 0), 0.0)
            average_ref[which, 8 * k : 8 * k + 8, :] = part * scale


def solution(mesh):
    sizes = tuple(mesh.shape[a] for a in ("gx", "gy", "row"))
    nrow = sizes[2]

    def per_device(occupancy, random_draws):
        any_space = pl.BlockSpec(memory_space=pl.ANY)
        vmem = pl.BlockSpec(memory_space=pltpu.VMEM)
        averages = pl.pallas_call(
            functools.partial(kernel, sizes),
            name="burst",
            out_shape=pltpu.VMEM((2, 32, 128), F32),
            in_specs=[any_space, any_space],
            out_specs=vmem,
            scratch_shapes=[
                pltpu.VMEM((8, 128, 512), jnp.int32),
                pltpu.VMEM((4, 8, 128, 512), BF16),
                pltpu.VMEM((2, 4, 4, 144, 128), F32),
                pltpu.VMEM((2, 4, 4, 4, 8, 128), F32),
                pltpu.VMEM((4, 4, 128, 128), F32),
                pltpu.VMEM((2, 4, 4, 40, 128), F32),
                pltpu.VMEM((3, 4, 4, 8, 128), F32),
                pltpu.VMEM((4, 2, 8, 512), F32),
                pltpu.VMEM((2, 160, 128), F32),
                pltpu.VMEM((4, 144, 128), F32),
                pltpu.VMEM((2, 1024, 128), BF16),
                pltpu.VMEM((2, 512, 128), BF16),
                pltpu.VMEM((2, 128, 128), BF16),
                pltpu.VMEM((5, 128, 128), BF16),
                pltpu.VMEM((2, 128, 128), BF16),
                pltpu.VMEM((2, 2, 128, 128), BF16),
                pltpu.VMEM((2, 2, 8, 128), BF16),
                pltpu.VMEM((4, 2, 8, 128), BF16),
                pltpu.VMEM((2, 37, 8, 128), BF16),
                pltpu.VMEM((2, 37, 8, 128), BF16),
                pltpu.VMEM((2, 32, 128), F32),
                pltpu.VMEM((nrow - 1, 2, 32, 128), F32),
                pltpu.VMEM((2, 8, 128), F32),
                pltpu.VMEM((nrow - 1, 2, 8, 128), F32),
                pltpu.SemaphoreType.DMA((20,)),
                pltpu.SemaphoreType.DMA((8,)),
                pltpu.SemaphoreType.DMA((8,)),
                pltpu.SemaphoreType.DMA((2, nrow - 1)),
                pltpu.SemaphoreType.DMA((2, nrow - 1)),
            ],
            compiler_params=pltpu.CompilerParams(
                collective_id=0, has_side_effects=True, vmem_limit_bytes=62 * 1024 * 1024
            ),
        )(occupancy, random_draws)
        coverage = averages[1]
        return coverage, coverage + (LEAP / 2.0) * (coverage - averages[0])

    return jax.shard_map(
        per_device,
        mesh=mesh,
        in_specs=(P("row", "gx", "gy"), P(None, "row", "gx", "gy")),
        out_specs=(P("gx", "gy"), P("gx", "gy")),
        check_vma=False,
    )
```
